256 devices in a mesh: ctx: 64 (over x, y_lo, z), rep: 4 (over y_hi, core).
Axes of the slice: x: 4, y: 4 (y_hi: 2, y_lo: 2; y = y_hi * 2 + y_lo), z: 8, core: 2. Of those that a mesh axis runs over, the one named last changes fastest.
Arguments:
- tokens: bfloat16 [4, 8192, 2880], P('rep', 'ctx'), may hold values from -6 to 6
- router_w: bfloat16 [2880, 32], replicated, may hold values from -0.109375 to 0.109375
- router_b: float32 [32], replicated, may hold values from -4 to 4
- hidden: bfloat16 [4, 8192, 4, 1536], P('rep', 'ctx'), may hold values from -6 to 6
- teacher_idx: int32 [4, 8192, 4], P('rep', 'ctx'), may hold values from 0 to 31, all different within a row
- merge_map: int32 [32], replicated, may hold values from 0 to 15, as said below
- merge_coef: float32 [32], replicated, may hold values from 0.3 to 1.5
- source_w: bfloat16 [32, 1536, 1536], P(None, 'ctx'), may hold values from -0.15625 to 0.15625
- out_grad: bfloat16 [4, 8192, 1536], P('rep', 'ctx'), may hold values from -6 to 6
Outputs:
- mixed: bfloat16 [4, 8192, 1536], P('rep', 'ctx')
- hidden_grad: bfloat16 [4, 8192, 4, 1536], P('rep', 'ctx')
- token_grad: bfloat16 [4, 8192, 2880], P('rep', 'ctx')
- router_w_grad: float32 [2880, 32], replicated
- router_b_grad: float32 [32], replicated
- coef_grad: float32 [32], replicated
- source_w_grad: float32 [32, 1536, 1536], P(None, 'ctx', 'rep')
The draws below stay inside these ranges and needn't reach their ends.
Inputs may be any that keep to these rules, and one draw needn't show every extreme that they name: `teacher_idx`: each token names 4 different experts. `merge_map`: each of the 16 combinations takes exactly two of the 32 experts.
All inputs are finite; a program needn't handle non-finite values.
Results may differ from the reference program's by a relative error of at most 0.0064.
Values may be sent and summed in bfloat16 or wider, within the bound.
A program may use at most 128 MiB of HBM per device.

```python
import math
import jax
import jax.numpy as jnp
from jax import lax

D = 2880
SOURCES = 32
TOP = 4
MERGED = 16
DW = 1536
FFW = 1536
TOK_DEV = 128
SEQS = 4
LENGTH = 8192
LOCAL_M = 1
COPIES = 4
CAP = 10
ALL_TOK = 32768
N_CTX = 64


def draw_merge_map(key, part):
    order = jax.random.permutation(jax.random.fold_in(key, 11), SOURCES)
    return (order // 2).astype(jnp.int32)


def block_scale(stream_key, dims, split, smallest, largest):
    loudness, own = 1.0, jax.random.fold_in(stream_key, 6)
    for dim, shards_of in split:
        steps = jnp.exp(jax.random.uniform(jax.random.fold_in(own, dim), (shards_of,), jnp.float32, smallest / len(split), largest / len(split)))
        loudness = loudness * jnp.repeat(steps, dims[dim] // shards_of).reshape([-1 if axis == dim else 1 for axis in range(len(dims))])
    return loudness


def distinct(stream_key, rows, number_of, top, lift):
    sequence = jax.random.permutation(jax.random.fold_in(stream_key, 1), number_of)
    boost = sequence
    for power in range(3):
        boost = boost * boost // number_of
    boost = boost * lift // number_of
    lots = jax.random.randint(jax.random.fold_in(stream_key, 2), (rows, number_of), 0, 4096) + boost
    holders = jax.random.permutation(jax.random.fold_in(stream_key, 3), rows)[jnp.arange(number_of) % rows]
    lots = jnp.where(jnp.arange(rows)[:, None] == holders[None, :], 1 << 14, lots)
    merit = lots * number_of + jnp.arange(number_of)
    return lax.top_k(merit.astype(jnp.int32), top)[1].astype(jnp.int32)


def normal_values(stream_key, dims, spread, bound, cuts=(), held_as=jnp.bfloat16):
    loudness = block_scale(stream_key, dims, cuts, -0.22, 0.18) if cuts else 1.0
    drawn = jax.random.normal(stream_key, dims, jnp.float32) * spread * loudness
    return jnp.minimum(jnp.maximum(drawn, -bound), bound).astype(held_as)


def setup_inputs(seed: int = 0) -> dict:
    splits = jax.random.split(jax.random.key(seed), 10)
    tokens = normal_values(splits[0], (SEQS, LENGTH, D), 1.0, 6.0, ((0, 4), (1, 64)))
    router_w = normal_values(splits[1], (D, SOURCES), D ** -0.5, 0.109375)
    router_b = normal_values(splits[2], (SOURCES,), 1.0, 4.0, (), jnp.float32)
    hidden = normal_values(splits[3], (SEQS, LENGTH, TOP, FFW), 1.0, 6.0, ((0, 4), (1, 64)))
    teacher_idx = distinct(splits[4], SEQS * LENGTH, SOURCES, TOP, 0).reshape((SEQS, LENGTH, TOP))
    merge_map = draw_merge_map(jax.random.fold_in(splits[9], 71), 0)
    merge_coef = jnp.clip(jnp.exp(jax.random.uniform(splits[6], (SOURCES,), jnp.float32, math.log(0.3), math.log(1.5))), 0.3, 1.5)
    source_w = normal_values(splits[7], (SOURCES, DW, FFW), FFW ** -0.5, 0.15625, ((1, 64),))
    out_grad = normal_values(splits[8], (SEQS, LENGTH, DW), 1.0, 6.0, ((0, 4), (1, 64)))
    return dict(tokens=tokens, router_w=router_w, router_b=router_b, hidden=hidden, teacher_idx=teacher_idx, merge_map=merge_map, merge_coef=merge_coef, source_w=source_w, out_grad=out_grad)


def reference(tokens, router_w, router_b, hidden, teacher_idx, merge_map, merge_coef, source_w, out_grad):
    seq_count = tokens.shape[0]
    seq_len = tokens.shape[1]
    blocks = seq_count * N_CTX
    per_block = TOK_DEV * TOP
    grad_scale = 1.0 / math.sqrt(ALL_TOK)
    flat_x = tokens.reshape(-1, D)
    logits = jnp.dot(flat_x, router_w, preferred_element_type=jnp.float32) + router_b
    choice_ids = teacher_idx.reshape(-1, TOP)
    chosen = jnp.take_along_axis(logits, choice_ids, axis=1)
    raised = jnp.exp(chosen)
    gate_probs = raised / lax.optimization_barrier(jnp.sum(raised, axis=1, keepdims=True))
    merged_id = merge_map[choice_ids]
    position = jnp.tile(jnp.arange(seq_len, dtype=jnp.int32), seq_count)
    lane_id = merged_id // LOCAL_M * COPIES + (position % COPIES)[:, None]
    member_id = merged_id % LOCAL_M
    lane_blocks = lane_id.reshape(blocks, per_block)
    onehot = (lane_blocks[:, :, None] == jnp.arange(N_CTX, dtype=jnp.int32)[None, None, :]).astype(jnp.int32)
    before = jnp.cumsum(onehot, axis=1) - onehot
    slot_rank = lax.optimization_barrier(jnp.sum(before * onehot, axis=2))
    is_kept = slot_rank < CAP
    slot_index = jnp.where(is_kept, lane_blocks * CAP + slot_rank, N_CTX * CAP)
    block_ids = jnp.broadcast_to(jnp.arange(blocks, dtype=jnp.int32)[:, None], (blocks, per_block))
    slot_numbers = jnp.broadcast_to(jnp.arange(per_block, dtype=jnp.int32)[None, :], (blocks, per_block))
    slot_source = jnp.full((blocks, N_CTX * CAP + 1), per_block, jnp.int32)
    slot_source = slot_source.at[block_ids, slot_index].set(slot_numbers)
    slot_source = slot_source[:, :N_CTX * CAP].reshape(blocks, N_CTX, CAP)
    slot_grad = (gate_probs[:, :, None] * out_grad.reshape(-1, 1, DW).astype(jnp.float32)).astype(jnp.bfloat16)
    pad_hidden = jnp.concatenate([hidden.reshape(blocks, per_block, FFW), jnp.zeros((blocks, 1, FFW), jnp.bfloat16)], axis=1)
    pad_grad = jnp.concatenate([slot_grad.reshape(blocks, per_block, DW), jnp.zeros((blocks, 1, DW), jnp.bfloat16)], axis=1)
    pad_member = jnp.concatenate([member_id.reshape(blocks, per_block), jnp.zeros((blocks, 1), jnp.int32)], axis=1)
    mixing = (merge_map[:, None] == jnp.arange(MERGED, dtype=jnp.int32)[None, :]).astype(jnp.float32) * merge_coef[:, None]
    merged = jnp.einsum('eg,edf->gdf', mixing, source_w.astype(jnp.float32), precision=lax.Precision.HIGHEST).astype(jnp.bfloat16)

    def lane_work(lane_now):
        source_now = lax.dynamic_index_in_dim(slot_source, lane_now, 1, keepdims=False)
        rows_hidden = jnp.take_along_axis(pad_hidden, source_now[:, :, None], axis=1).reshape(-1, FFW)
        rows_grad = jnp.take_along_axis(pad_grad, source_now[:, :, None], axis=1).reshape(-1, DW)
        rows_member = jnp.take_along_axis(pad_member, source_now, axis=1).reshape(-1)
        out_rows = jnp.zeros((rows_hidden.shape[0], DW), jnp.float32)
        back_rows = jnp.zeros((rows_hidden.shape[0], FFW), jnp.float32)
        grad_list = []
        for member_now in range(LOCAL_M):
            weight = lax.dynamic_index_in_dim(merged, lane_now // COPIES * LOCAL_M + member_now, 0, keepdims=False)
            selected = (rows_member == member_now)[:, None]
            forward = lax.dot_general(rows_hidden, weight, (((1,), (1,)), ((), ())), preferred_element_type=jnp.float32)
            out_rows = jnp.where(selected, forward, out_rows)
            backward = jnp.dot(rows_grad, weight, preferred_element_type=jnp.float32)
            back_rows = jnp.where(selected, backward, back_rows)
            masked = jnp.where(selected, rows_grad, jnp.zeros_like(rows_grad))
            grad_list.append(lax.dot_general(masked, rows_hidden, (((0,), (0,)), ((), ())), preferred_element_type=jnp.float32))
        return (out_rows.astype(jnp.bfloat16).reshape(blocks, CAP, DW), back_rows.astype(jnp.bfloat16).reshape(blocks, CAP, FFW), jnp.stack(grad_list))
    lane_out, lane_back, lane_grads = lax.map(lane_work, jnp.arange(N_CTX, dtype=jnp.int32))
    merged_grad = lane_grads.reshape(MERGED // LOCAL_M, COPIES, LOCAL_M, DW, FFW).sum(axis=1).reshape(MERGED, DW, FFW)
    lane_safe = jnp.where(is_kept, lane_blocks, 0)
    rank_safe = jnp.where(is_kept, slot_rank, 0)
    slot_out = jnp.where(is_kept[:, :, None], lane_out[lane_safe, block_ids, rank_safe], jnp.zeros((), jnp.bfloat16)).reshape(-1, TOP, DW)
    hidden_grad = jnp.where(is_kept[:, :, None], lane_back[lane_safe, block_ids, rank_safe], jnp.zeros((), jnp.bfloat16)).reshape(seq_count, seq_len, TOP, FFW)
    mixed = lax.optimization_barrier(jnp.sum(gate_probs[:, :, None] * slot_out.astype(jnp.float32), axis=1)).astype(jnp.bfloat16).reshape(seq_count, seq_len, DW)
    score_grad = lax.optimization_barrier(jnp.sum(out_grad.reshape(-1, 1, DW).astype(jnp.float32) * slot_out.astype(jnp.float32), axis=2))
    chosen_grad = gate_probs * (score_grad - lax.optimization_barrier(jnp.sum(gate_probs * score_grad, axis=1, keepdims=True)))
    pick_table = (choice_ids[:, :, None] == jnp.arange(SOURCES, dtype=jnp.int32)[None, None, :]).astype(jnp.float32)
    logit_grad = lax.optimization_barrier(jnp.sum(pick_table * chosen_grad[:, :, None], axis=1))
    logit_half = logit_grad.astype(jnp.bfloat16)
    token_grad = lax.dot_general(logit_half, router_w, (((1,), (1,)), ((), ())), preferred_element_type=jnp.float32).astype(jnp.bfloat16).reshape(seq_count, seq_len, D)
    router_w_grad = lax.dot_general(flat_x, logit_half, (((0,), (0,)), ((), ())), preferred_element_type=jnp.float32) * grad_scale
    router_b_grad = lax.optimization_barrier(jnp.sum(logit_grad, axis=0)) * grad_scale
    source_grad = merged_grad[merge_map]
    coef_grad = jnp.einsum('edf,edf->e', source_grad, source_w.astype(jnp.float32), precision=lax.Precision.HIGHEST) * grad_scale
    source_w_grad = source_grad * merge_coef[:, None, None] * grad_scale
    return (mixed, hidden_grad, token_grad, router_w_grad, router_b_grad, coef_grad, source_w_grad)
```

```python
import math

import jax
import jax.numpy as jnp
from jax import lax
from jax.sharding import PartitionSpec as P

PLANE = ("x", "yh", "yl")


def on_device(
    tokens, router_w, router_b, hidden, teacher_idx, merge_map, merge_coef, source_w, out_grad
):
    tok, feat = tokens.shape[1], tokens.shape[2]
    top, ffw = teacher_idx.shape[2], hidden.shape[3]
    dw = out_grad.shape[2]
    experts = router_w.shape[1]
    groups = 16
    copies = 4
    cap = 10
    slots = tok * top
    rows = 64 * cap
    quarter = ffw // 4
    grad_scale = 1.0 / math.sqrt(tok * 256)
    c, yh = lax.axis_index("c"), lax.axis_index("yh")
    x = tokens.reshape(tok, feat)
    hid = hidden.reshape(slots, ffw)
    og = out_grad.reshape(tok, dw)
    logits = jnp.dot(x, router_w, preferred_element_type=jnp.float32) + router_b
    choice = teacher_idx.reshape(tok, top)
    pick = choice[:, :, None] == jnp.arange(experts, dtype=jnp.int32)
    pick_float = pick.astype(jnp.float32)
    chosen = jnp.sum(pick_float * logits[:, None, :], axis=2)
    raised = jnp.exp(chosen)
    gate = raised / jnp.sum(raised, axis=1, keepdims=True)
    merged_id = jnp.sum(jnp.where(pick, merge_map[None, None, :], 0), axis=2)
    lane = (merged_id * copies + (jnp.arange(tok, dtype=jnp.int32) % copies)[:, None]).reshape(-1)
    onehot = (lane[:, None] == jnp.arange(64, dtype=jnp.int32)[None, :]).astype(jnp.bfloat16)
    lower = (
        jnp.arange(slots)[:, None] > jnp.arange(slots)[None, :]
    ).astype(jnp.bfloat16)
    before = jnp.dot(lower, onehot, preferred_element_type=jnp.float32)
    rank = jnp.sum(before * onehot.astype(jnp.float32), axis=1).astype(jnp.int32)
    index = jnp.where(rank < cap, lane * cap + rank, rows)
    select = (index[None, :] == jnp.arange(rows, dtype=jnp.int32)[:, None]).astype(jnp.bfloat16)
    slot_grad = (gate[:, :, None] * og[:, None, :]).astype(jnp.bfloat16).reshape(slots, dw)
    send_h = jnp.dot(select, hid, preferred_element_type=jnp.float32).astype(jnp.bfloat16)
    send_g = jnp.dot(select, slot_grad, preferred_element_type=jnp.float32).astype(jnp.bfloat16)

    ids = jnp.arange(experts, dtype=jnp.int32)
    same = merge_map[:, None] == merge_map[None, :]
    second = jnp.any(same & (ids[:, None] > ids[None, :]), axis=1)
    member = merge_map[None, :] == jnp.arange(groups, dtype=jnp.int32)[:, None]
    first_id = jnp.sum(jnp.where(member & ~second[None, :], ids[None, :], 0), axis=1)
    second_id = jnp.sum(jnp.where(member & second[None, :], ids[None, :], 0), axis=1)
    mine = lax.dynamic_slice_in_dim(source_w, (c * 2 + yh) * quarter, quarter, 2)
    merged = (
        merge_coef[first_id][:, None, None] * mine[first_id].astype(jnp.float32)
        + merge_coef[second_id][:, None, None] * mine[second_id].astype(jnp.float32)
    ).astype(jnp.bfloat16)
    share = source_w.shape[1]

    part = lax.all_to_all(merged, PLANE, 0, 0, tiled=True)
    full = lax.all_gather(part, ("z", "c"))
    weight = (
        full.reshape(8, 2, 4, 2, 2, share, quarter)
        .transpose(2, 4, 0, 5, 1, 3, 6)
        .reshape(dw, ffw)
    )
    got_h = lax.all_to_all(send_h.reshape(groups, -1, ffw), PLANE, 0, 0, tiled=True)
    got_g = lax.all_to_all(send_g.reshape(groups, -1, dw), PLANE, 0, 0, tiled=True)
    got_h = got_h.reshape(rows, ffw)
    got_g = got_g.reshape(rows, dw)
    out_rows = lax.dot_general(
        got_h, weight, (((1,), (1,)), ((), ())), preferred_element_type=jnp.float32
    ).astype(jnp.bfloat16)
    back_rows = jnp.dot(got_g, weight, preferred_element_type=jnp.float32).astype(jnp.bfloat16)
    lane_grad = lax.dot_general(
        got_g, got_h, (((0,), (0,)), ((), ())), preferred_element_type=jnp.float32
    )
    home_out = lax.all_to_all(out_rows.reshape(groups, -1, dw), PLANE, 0, 0, tiled=True)
    home_back = lax.all_to_all(back_rows.reshape(groups, -1, ffw), PLANE, 0, 0, tiled=True)
    home_out = home_out.reshape(rows, dw)
    home_back = home_back.reshape(rows, ffw)
    pieces = (
        lane_grad.reshape(4, 2, 8, share, 2, 2, quarter)
        .transpose(2, 5, 0, 4, 1, 3, 6)
        .reshape(16, 16 * share, quarter)
    )
    summed = lax.psum_scatter(pieces, ("z", "c"), scatter_dimension=0, tiled=False)
    merged_grad = lax.all_to_all(
        summed.reshape(groups, share, quarter), PLANE, 0, 0, tiled=True
    )

    spread = (
        index[:, None] == jnp.arange(rows, dtype=jnp.int32)[None, :]
    ).astype(jnp.bfloat16)
    slot_out = jnp.dot(spread, home_out, preferred_element_type=jnp.float32)
    slot_out = slot_out.reshape(tok, top, dw)
    hidden_grad = (
        jnp.dot(spread, home_back, preferred_element_type=jnp.float32)
        .astype(jnp.bfloat16)
        .reshape(1, tok, top, ffw)
    )
    mixed = jnp.sum(gate[:, :, None] * slot_out, axis=1).astype(jnp.bfloat16)
    score = jnp.sum(og[:, None, :].astype(jnp.float32) * slot_out, axis=2)
    chosen_grad = gate * (score - jnp.sum(gate * score, axis=1, keepdims=True))
    logit_grad = jnp.sum(pick_float * chosen_grad[:, :, None], axis=1)
    logit_half = logit_grad.astype(jnp.bfloat16)
    token_grad = lax.dot_general(
        logit_half, router_w, (((1,), (1,)), ((), ())), preferred_element_type=jnp.float32
    ).astype(jnp.bfloat16)
    part_w = lax.dot_general(
        x, logit_half, (((0,), (0,)), ((), ())), preferred_element_type=jnp.float32
    )
    part_b = jnp.sum(logit_grad, axis=0)
    source_grad = merged_grad[merge_map]
    mine_out = lax.dynamic_slice_in_dim(source_w, (yh * 2 + c) * quarter, quarter, 2)
    part_c = jnp.sum(source_grad * mine_out.astype(jnp.float32), axis=(1, 2))
    source_w_grad = source_grad * (merge_coef * grad_scale)[:, None, None]
    every = ("x", "yl", "z", "yh", "c")
    sum_w, sum_b, sum_c = lax.psum((part_w, part_b, part_c), every)
    return (
        mixed.reshape(1, tok, dw),
        hidden_grad,
        token_grad.reshape(1, tok, feat),
        sum_w * grad_scale,
        sum_b * grad_scale,
        sum_c * grad_scale,
        source_w_grad,
    )


def solution(mesh):
    fine = jax.sharding.Mesh(mesh.devices.reshape(4, 2, 8, 2, 2), ("x", "yl", "z", "yh", "c"))
    ctx, rep = ("x", "yl", "z"), ("yh", "c")
    in_specs = (
        P(rep, ctx, None),
        P(),
        P(),
        P(rep, ctx, None, None),
        P(rep, ctx, None),
        P(),
        P(),
        P(None, ctx, None),
        P(rep, ctx, None),
    )
    out_specs = (
        P(rep, ctx, None),
        P(rep, ctx, None, None),
        P(rep, ctx, None),
        P(),
        P(),
        P(),
        P(None, ctx, rep),
    )
    return jax.shard_map(
        on_device, mesh=fine, in_specs=in_specs, out_specs=out_specs, check_vma=False
    )
```

```python
import math

import jax
import jax.numpy as jnp
from jax import lax
from jax.experimental import pallas as pl
from jax.experimental.pallas import tpu as pltpu
from jax.sharding import PartitionSpec as P

MESH = pl.DeviceIdType.MESH
BF = jnp.bfloat16
F32 = jnp.float32


def offset(k, x, y):
    px = lax.rem(x + k // 4, 4)
    py = lax.rem(y + lax.rem(k, 4), 4)
    return px, py


def plane_id(px, py):
    return {"x": px, "yl": lax.rem(py, 2), "yh": py // 2}


def remote(src, dst, send, recv, where):
    return pltpu.make_async_remote_copy(
        src_ref=src, dst_ref=dst, send_sem=send, recv_sem=recv, device_id=where,
        device_id_type=MESH,
    )


def core_kernel(
    wq, send_h, send_g, home_out, home_back, grad_out,
    weight, recv_h, recv_g, mat_h, mat_g, mat_w, out_send, back_send,
    part, sib, ring_send, ring_recv, last,
    a_s, a_r, h_s, h_r, g_s, g_r, zp_s, zp_r, zm_s, zm_r, w_s, w_r,
    o_s, o_r, b_s, b_r, e_s, e_r, rp_s, rp_r, rm_s, rm_r, l_s, l_r,
):
    x, yl, z = lax.axis_index("x"), lax.axis_index("yl"), lax.axis_index("z")
    yh, c = lax.axis_index("yh"), lax.axis_index("c")
    y = yh * 2 + yl
    me = x * 4 + y
    xy = x * 2 + yl
    up, down = lax.rem(z + 1, 8), lax.rem(z + 7, 8)
    sibling = {"c": 1 - c}

    barrier = pltpu.get_barrier_semaphore()

    def greet(k, carry):
        px, py = offset(k, x, y)
        pl.semaphore_signal(barrier, inc=1, device_id=plane_id(px, py), device_id_type=MESH)
        return carry

    lax.fori_loop(1, 16, greet, 0)
    for where in ({"z": up}, {"z": down}, sibling):
        pl.semaphore_signal(barrier, inc=1, device_id=where, device_id_type=MESH)
    pl.semaphore_wait(barrier, 18)

    quarter = pl.ds(pl.multiple_of((c * 2 + yh) * 384, 384), 384)
    half = pl.ds(pl.multiple_of(c * 768, 768), 768)

    def a_copy(k):
        px, py = offset(k, x, y)
        return remote(
            wq.at[px * 4 + py], weight.at[xy, z, :, :, quarter], a_s.at[k], a_r.at[k],
            plane_id(px, py),
        )

    def h_copy(k):
        px, py = offset(k, x, y)
        return remote(
            send_h.at[pl.ds(5 * (px * 4 + py), 5)], recv_h.at[pl.ds(5 * me, 5)],
            h_s.at[k], h_r.at[k], plane_id(px, py),
        )

    def g_copy(k):
        px, py = offset(k, x, y)
        return remote(
            send_g.at[pl.ds(5 * (px * 4 + py), 5)], recv_g.at[pl.ds(5 * me, 5)],
            g_s.at[k], g_r.at[k], plane_id(px, py),
        )

    def o_copy(k):
        px, py = offset(k, x, y)
        return remote(
            out_send.at[pl.ds(5 * (px * 4 + py), 5)], home_out.at[pl.ds(5 * me, 5)],
            o_s.at[k], o_r.at[k], plane_id(px, py),
        )

    def b_copy(k):
        px, py = offset(k, x, y)
        return remote(
            back_send.at[pl.ds(5 * (px * 4 + py), 5)], home_back.at[pl.ds(5 * me, 5)],
            b_s.at[k], b_r.at[k], plane_id(px, py),
        )

    def l_copy(k):
        px, py = offset(k, x, y)
        return remote(
            last.at[py // 2, px * 2 + lax.rem(py, 2)], grad_out.at[me],
            l_s.at[k], l_r.at[k], plane_id(px, py),
        )

    def each(do):
        def step(k, carry):
            do(k)
            return carry

        lax.fori_loop(1, 16, step, 0)

    each(lambda k: a_copy(k).start())
    each(lambda k: h_copy(k).start())
    each(lambda k: g_copy(k).start())
    own = pl.ds(5 * me, 5)
    weight[xy, z, :, :, quarter] = wq[me]
    recv_h[own] = send_h[own]
    recv_g[own] = send_g[own]
    each(lambda k: a_copy(k).wait_recv())

    def block(b):
        return weight.at[:, b, :, :, half]

    def w_copy(i):
        b = lax.rem(z + 8 - i, 8) if i <= 4 else lax.rem(z + i - 4, 8)
        return remote(block(b), block(b), w_s.at[i], w_r.at[i], sibling)

    def zp_copy(s):
        b = lax.rem(z + 8 - s, 8)
        return remote(block(b), block(b), zp_s.at[s], zp_r.at[s], {"z": up})

    def zm_copy(s):
        b = lax.rem(z + s, 8)
        return remote(block(b), block(b), zm_s.at[s], zm_r.at[s], {"z": down})

    zp_copy(0).start()
    zm_copy(0).start()
    w_copy(0).start()
    for s in range(4):
        zp_copy(s).wait_recv()
        if s < 3:
            zp_copy(s + 1).start()
        w_copy(s + 1).start()
        if s < 3:
            zm_copy(s).wait_recv()
            if s < 2:
                zm_copy(s + 1).start()
            w_copy(s + 5).start()

    each(lambda k: h_copy(k).wait_recv())

    def shape_h(i, carry):
        mat_h[pl.ds(pl.multiple_of(i * 80, 80), 80), :] = (
            recv_h[pl.ds(i * 10, 10)].astype(F32).reshape(80, 1536).astype(BF)
        )
        return carry

    lax.fori_loop(0, 8, shape_h, 0)
    each(lambda k: g_copy(k).wait_recv())

    def shape_g(i, carry):
        mat_g[pl.ds(pl.multiple_of(i * 80, 80), 80), :] = (
            recv_g[pl.ds(i * 10, 10)].astype(F32).reshape(80, 1536).astype(BF)
        )
        return carry

    lax.fori_loop(0, 8, shape_g, 0)

    def outer(i, carry):
        cols = pl.ds(pl.multiple_of(i * 384, 384), 384)
        tile = lax.dot_general(
            mat_g[:, cols], mat_h[...], (((0,), (0,)), ((), ())), preferred_element_type=F32
        )
        part[pl.ds(i * 2, 2)] = tile.reshape(2, 8, 3, 8, 1536).astype(BF)
        return carry

    lax.fori_loop(0, 4, outer, 0)

    def e_copy(h):
        there = pl.ds(pl.multiple_of(h * 768 + (1 - c) * 384, 384), 384)
        return remote(
            part.at[:, :, :, :, there], sib.at[h], e_s.at[h], e_r.at[h], sibling
        )

    for h in range(2):
        e_copy(h).start()
    for i in range(8):
        w_copy(i).wait_recv()

    def shape_w(i, carry):
        mat_w[pl.ds(pl.multiple_of(i * 192, 192), 192), :] = (
            weight[i].astype(F32).reshape(192, 1536).astype(BF)
        )
        return carry

    lax.fori_loop(0, 8, shape_w, 0)

    def forward(j, carry):
        span = pl.ds(pl.multiple_of(j * 256, 256), 256)
        tile = lax.dot_general(
            mat_h[...], mat_w[span, :], (((1,), (1,)), ((), ())), preferred_element_type=F32
        )
        out_send[:, :, span] = tile.reshape(80, 8, 256).astype(BF)
        return carry

    lax.fori_loop(0, 6, forward, 0)
    each(lambda k: o_copy(k).start())
    home_out[own] = out_send[own]

    def backward(j, carry):
        span = pl.ds(pl.multiple_of(j * 256, 256), 256)
        tile = jnp.dot(mat_g[...], mat_w[:, span], preferred_element_type=F32)
        back_send[:, :, span] = tile.reshape(80, 8, 256).astype(BF)
        return carry

    lax.fori_loop(0, 6, backward, 0)
    each(lambda k: b_copy(k).start())
    home_back[own] = back_send[own]

    for h in range(2):
        e_copy(h).wait_recv()

    def local(h, b):
        here = pl.ds(pl.multiple_of(h * 768 + c * 384, 384), 384)
        return part[:, b, :, :, here].astype(F32) + sib[h, :, b].astype(F32)

    def ring(h, s):
        if h == 0:
            return remote(
                ring_send.at[0, s], ring_recv.at[0, s], rp_s.at[s], rp_r.at[s], {"z": up}
            )
        return remote(
            ring_send.at[1, s], ring_recv.at[1, s], rm_s.at[s], rm_r.at[s], {"z": down}
        )

    for s in range(7):
        for h in range(2):
            b = lax.rem(z + 15 - s, 8) if h == 0 else lax.rem(z + 1 + s, 8)
            total = local(h, b)
            if s > 0:
                ring(h, s - 1).wait_recv()
                total = total + ring_recv[h, s - 1].astype(F32)
            ring_send[h, s] = total.astype(BF)
            ring(h, s).start()
    for h in range(2):
        total = local(h, z)
        ring(h, 6).wait_recv()
        last[h] = total + ring_recv[h, 6].astype(F32)
    each(lambda k: l_copy(k).start())
    grad_out[me] = last[yh, xy]

    each(lambda k: a_copy(k).wait_send())
    each(lambda k: h_copy(k).wait_send())
    each(lambda k: g_copy(k).wait_send())
    for s in range(4):
        zp_copy(s).wait_send()
    for s in range(3):
        zm_copy(s).wait_send()
    for i in range(8):
        w_copy(i).wait_send()
    for h in range(2):
        e_copy(h).wait_send()
        for s in range(7):
            ring(h, s).wait_send()
    each(lambda k: o_copy(k).wait())
    each(lambda k: b_copy(k).wait())
    each(lambda k: l_copy(k).wait())


def exchange(wq, send_h, send_g):
    vmem = pl.BlockSpec(memory_space=pltpu.VMEM)
    dma = lambda n: pltpu.SemaphoreType.DMA((n,))
    rows = pltpu.VMEM((80, 8, 1536), BF)
    mat = pltpu.VMEM((640, 1536), BF)
    return pl.pallas_call(
        core_kernel,
        out_shape=(
            jax.ShapeDtypeStruct((80, 8, 1536), BF),
            jax.ShapeDtypeStruct((80, 8, 1536), BF),
            jax.ShapeDtypeStruct((16, 3, 8, 384), F32),
        ),
        in_specs=[vmem] * 3,
        out_specs=(vmem,) * 3,
        scratch_shapes=[
            pltpu.VMEM((8, 8, 3, 8, 1536), BF),
            rows, rows, mat, mat,
            pltpu.VMEM((1536, 1536), BF),
            rows, rows,
            pltpu.VMEM((8, 8, 3, 8, 1536), BF),
            pltpu.VMEM((2, 8, 8, 3, 8, 384), BF),
            pltpu.VMEM((2, 7, 8, 3, 8, 384), BF),
            pltpu.VMEM((2, 7, 8, 3, 8, 384), BF),
            pltpu.VMEM((2, 8, 3, 8, 384), F32),
            dma(16), dma(16), dma(16), dma(16), dma(16), dma(16),
            dma(4), dma(4), dma(3), dma(3), dma(8), dma(8),
            dma(16), dma(16), dma(16), dma(16), dma(2), dma(2),
            dma(7), dma(7), dma(7), dma(7), dma(16), dma(16),
        ],
        compiler_params=pltpu.CompilerParams(
            collective_id=0, has_side_effects=True, vmem_limit_bytes=64000000
        ),
        name="exchange",
    )(wq, send_h, send_g)


def on_device(
    tokens, router_w, router_b, hidden, teacher_idx, merge_map, merge_coef, source_w, out_grad
):
    tok, feat = tokens.shape[1], tokens.shape[2]
    top, ffw = teacher_idx.shape[2], hidden.shape[3]
    dw = out_grad.shape[2]
    experts = router_w.shape[1]
    groups = 16
    copies = 4
    cap = 10
    slots = tok * top
    rows = 64 * cap
    quarter = ffw // 4
    grad_scale = 1.0 / math.sqrt(tok * 256)
    c, yh = lax.axis_index("c"), lax.axis_index("yh")
    x = tokens.reshape(tok, feat)
    hid = hidden.reshape(slots, ffw)
    og = out_grad.reshape(tok, dw)
    logits = jnp.dot(x, router_w, preferred_element_type=jnp.float32) + router_b
    choice = teacher_idx.reshape(tok, top)
    pick = choice[:, :, None] == jnp.arange(experts, dtype=jnp.int32)
    pick_float = pick.astype(jnp.float32)
    chosen = jnp.sum(pick_float * logits[:, None, :], axis=2)
    raised = jnp.exp(chosen)
    gate = raised / jnp.sum(raised, axis=1, keepdims=True)
    merged_id = jnp.sum(jnp.where(pick, merge_map[None, None, :], 0), axis=2)
    lane = (merged_id * copies + (jnp.arange(tok, dtype=jnp.int32) % copies)[:, None]).reshape(-1)
    onehot = (lane[:, None] == jnp.arange(64, dtype=jnp.int32)[None, :]).astype(jnp.bfloat16)
    lower = (
        jnp.arange(slots)[:, None] > jnp.arange(slots)[None, :]
    ).astype(jnp.bfloat16)
    before = jnp.dot(lower, onehot, preferred_element_type=jnp.float32)
    rank = jnp.sum(before * onehot.astype(jnp.float32), axis=1).astype(jnp.int32)
    index = jnp.where(rank < cap, lane * cap + rank, rows)
    select = (index[None, :] == jnp.arange(rows, dtype=jnp.int32)[:, None]).astype(jnp.bfloat16)
    slot_grad = (gate[:, :, None] * og[:, None, :]).astype(jnp.bfloat16).reshape(slots, dw)
    send_h = jnp.dot(select, hid, preferred_element_type=jnp.float32).astype(jnp.bfloat16)
    send_g = jnp.dot(select, slot_grad, preferred_element_type=jnp.float32).astype(jnp.bfloat16)

    ids = jnp.arange(experts, dtype=jnp.int32)
    same = merge_map[:, None] == merge_map[None, :]
    second = jnp.any(same & (ids[:, None] > ids[None, :]), axis=1)
    member = merge_map[None, :] == jnp.arange(groups, dtype=jnp.int32)[:, None]
    first_id = jnp.sum(jnp.where(member & ~second[None, :], ids[None, :], 0), axis=1)
    second_id = jnp.sum(jnp.where(member & second[None, :], ids[None, :], 0), axis=1)
    mine = lax.dynamic_slice_in_dim(source_w, (c * 2 + yh) * quarter, quarter, 2)
    merged = (
        merge_coef[first_id][:, None, None] * mine[first_id].astype(jnp.float32)
        + merge_coef[second_id][:, None, None] * mine[second_id].astype(jnp.float32)
    ).astype(jnp.bfloat16)
    share = source_w.shape[1]

    home_out, home_back, merged_grad = exchange(
        merged.reshape(groups, 3, 8, quarter),
        send_h.reshape(80, 8, ffw),
        send_g.reshape(80, 8, dw),
    )
    home_out = home_out.reshape(rows, dw)
    home_back = home_back.reshape(rows, ffw)
    merged_grad = merged_grad.reshape(groups, share, quarter)

    spread = (
        index[:, None] == jnp.arange(rows, dtype=jnp.int32)[None, :]
    ).astype(jnp.bfloat16)
    slot_out = jnp.dot(spread, home_out, preferred_element_type=jnp.float32)
    slot_out = slot_out.reshape(tok, top, dw)
    hidden_grad = (
        jnp.dot(spread, home_back, preferred_element_type=jnp.float32)
        .astype(jnp.bfloat16)
        .reshape(1, tok, top, ffw)
    )
    mixed = jnp.sum(gate[:, :, None] * slot_out, axis=1).astype(jnp.bfloat16)
    score = jnp.sum(og[:, None, :].astype(jnp.float32) * slot_out, axis=2)
    chosen_grad = gate * (score - jnp.sum(gate * score, axis=1, keepdims=True))
    logit_grad = jnp.sum(pick_float * chosen_grad[:, :, None], axis=1)
    logit_half = logit_grad.astype(jnp.bfloat16)
    token_grad = lax.dot_general(
        logit_half, router_w, (((1,), (1,)), ((), ())), preferred_element_type=jnp.float32
    ).astype(jnp.bfloat16)
    part_w = lax.dot_general(
        x, logit_half, (((0,), (0,)), ((), ())), preferred_element_type=jnp.float32
    )
    part_b = jnp.sum(logit_grad, axis=0)
    source_grad = merged_grad[merge_map]
    mine_out = lax.dynamic_slice_in_dim(source_w, (yh * 2 + c) * quarter, quarter, 2)
    part_c = jnp.sum(source_grad * mine_out.astype(jnp.float32), axis=(1, 2))
    source_w_grad = source_grad * (merge_coef * grad_scale)[:, None, None]
    every = ("x", "yl", "z", "yh", "c")
    sum_w, sum_b, sum_c = lax.psum((part_w, part_b, part_c), every)
    return (
        mixed.reshape(1, tok, dw),
        hidden_grad,
        token_grad.reshape(1, tok, feat),
        sum_w * grad_scale,
        sum_b * grad_scale,
        sum_c * grad_scale,
        source_w_grad,
    )


def solution(mesh):
    fine = jax.sharding.Mesh(mesh.devices.reshape(4, 2, 8, 2, 2), ("x", "yl", "z", "yh", "c"))
    ctx, rep = ("x", "yl", "z"), ("yh", "c")
    in_specs = (
        P(rep, ctx, None),
        P(),
        P(),
        P(rep, ctx, None, None),
        P(rep, ctx, None),
        P(),
        P(),
        P(None, ctx, None),
        P(rep, ctx, None),
    )
    out_specs = (
        P(rep, ctx, None),
        P(rep, ctx, None, None),
        P(rep, ctx, None),
        P(),
        P(),
        P(),
        P(None, ctx, rep),
    )
    return jax.shard_map(
        on_device, mesh=fine, in_specs=in_specs, out_specs=out_specs, check_vma=False
    )
```

```python
import math

import jax
import jax.numpy as jnp
from jax import lax
from jax.experimental import pallas as pl
from jax.experimental.pallas import tpu as pltpu
from jax.sharding import PartitionSpec as P

MESH = pl.DeviceIdType.MESH
BF = jnp.bfloat16
F32 = jnp.float32


def offset(k, x, y):
    px = lax.rem(x + k // 4, 4)
    py = lax.rem(y + lax.rem(k, 4), 4)
    return px, py


def plane_id(px, py):
    return {"x": px, "yl": lax.rem(py, 2), "yh": py // 2}


def remote(src, dst, send, recv, where):
    return pltpu.make_async_remote_copy(
        src_ref=src, dst_ref=dst, send_sem=send, recv_sem=recv, device_id=where,
        device_id_type=MESH,
    )


def core_kernel(
    wq, send_h, send_g, home_out, home_back, grad_out,
    weight, recv_h, recv_g, mat_h, mat_g, mat_w, out_send, back_send,
    part, sib, ring_send, ring_recv, last,
    a_s, a_r, h_s, h_r, g_s, g_r, zp_s, zp_r, zm_s, zm_r, w_s, w_r,
    o_s, o_r, b_s, b_r, e_s, e_r, rp_s, rp_r, rm_s, rm_r, l_s, l_r,
):
    x, yl, z = lax.axis_index("x"), lax.axis_index("yl"), lax.axis_index("z")
    yh, c = lax.axis_index("yh"), lax.axis_index("c")
    y = yh * 2 + yl
    me = x * 4 + y
    xy = x * 2 + yl
    up, down = lax.rem(z + 1, 8), lax.rem(z + 7, 8)
    sibling = {"c": 1 - c}

    barrier = pltpu.get_barrier_semaphore()

    def greet(k, carry):
        px, py = offset(k, x, y)
        pl.semaphore_signal(barrier, inc=1, device_id=plane_id(px, py), device_id_type=MESH)
        return carry

    lax.fori_loop(1, 16, greet, 0)
    for where in ({"z": up}, {"z": down}, sibling):
        pl.semaphore_signal(barrier, inc=1, device_id=where, device_id_type=MESH)
    pl.semaphore_wait(barrier, 18)

    quarter = pl.ds(pl.multiple_of((c * 2 + yh) * 384, 384), 384)
    half = pl.ds(pl.multiple_of(c * 768, 768), 768)

    def a_copy(k):
        px, py = offset(k, x, y)
        return remote(
            wq.at[px * 4 + py], weight.at[xy, z, :, :, quarter], a_s.at[k], a_r.at[k],
            plane_id(px, py),
        )

    def h_copy(k):
        px, py = offset(k, x, y)
        return remote(
            send_h.at[pl.ds(5 * (px * 4 + py), 5)], recv_h.at[pl.ds(5 * me, 5)],
            h_s.at[k], h_r.at[k], plane_id(px, py),
        )

    def g_copy(k):
        px, py = offset(k, x, y)
        return remote(
            send_g.at[pl.ds(5 * (px * 4 + py), 5)], recv_g.at[pl.ds(5 * me, 5)],
            g_s.at[k], g_r.at[k], plane_id(px, py),
        )

    def o_copy(k):
        px, py = offset(k, x, y)
        return remote(
            out_send.at[pl.ds(5 * (px * 4 + py), 5)], home_out.at[pl.ds(5 * me, 5)],
            o_s.at[k], o_r.at[k], plane_id(px, py),
        )

    def b_copy(k):
        px, py = offset(k, x, y)
        return remote(
            back_send.at[pl.ds(5 * (px * 4 + py), 5)], home_back.at[pl.ds(5 * me, 5)],
            b_s.at[k], b_r.at[k], plane_id(px, py),
        )

    def l_copy(k):
        px, py = offset(k, x, y)
        return remote(
            last.at[py // 2, px * 2 + lax.rem(py, 2)], grad_out.at[me],
            l_s.at[k], l_r.at[k], plane_id(px, py),
        )

    def each(do):
        def step(k, carry):
            do(k)
            return carry

        lax.fori_loop(1, 16, step, 0)

    each(lambda k: a_copy(k).start())
    each(lambda k: h_copy(k).start())
    each(lambda k: g_copy(k).start())
    own = pl.ds(5 * me, 5)
    weight[xy, z, :, :, quarter] = wq[me]
    recv_h[own] = send_h[own]
    recv_g[own] = send_g[own]
    each(lambda k: a_copy(k).wait_recv())

    def block(b):
        return weight.at[:, b, :, :, half]

    def w_copy(i):
        b = lax.rem(z + 8 - i, 8) if i <= 4 else lax.rem(z + i - 4, 8)
        return remote(block(b), block(b), w_s.at[i], w_r.at[i], sibling)

    def zp_copy(s):
        b = lax.rem(z + 8 - s, 8)
        return remote(block(b), block(b), zp_s.at[s], zp_r.at[s], {"z": up})

    def zm_copy(s):
        b = lax.rem(z + s, 8)
        return remote(block(b), block(b), zm_s.at[s], zm_r.at[s], {"z": down})

    zp_copy(0).start()
    zm_copy(0).start()
    w_copy(0).start()
    for s in range(4):
        zp_copy(s).wait_recv()
        if s < 3:
            zp_copy(s + 1).start()
        w_copy(s + 1).start()
        if s < 3:
            zm_copy(s).wait_recv()
            if s < 2:
                zm_copy(s + 1).start()
            w_copy(s + 5).start()

    each(lambda k: h_copy(k).wait_recv())

    def shape_h(i, carry):
        mat_h[pl.ds(pl.multiple_of(i * 80, 80), 80), :] = (
            recv_h[pl.ds(i * 10, 10)].astype(F32).reshape(80, 1536).astype(BF)
        )
        return carry

    lax.fori_loop(0, 8, shape_h, 0)
    each(lambda k: g_copy(k).wait_recv())

    def shape_g(i, carry):
        mat_g[pl.ds(pl.multiple_of(i * 80, 80), 80), :] = (
            recv_g[pl.ds(i * 10, 10)].astype(F32).reshape(80, 1536).astype(BF)
        )
        return carry

    lax.fori_loop(0, 8, shape_g, 0)

    def outer(i, carry):
        cols = pl.ds(pl.multiple_of(i * 384, 384), 384)
        tile = lax.dot_general(
            mat_g[:, cols], mat_h[...], (((0,), (0,)), ((), ())), preferred_element_type=F32
        )
        part[pl.ds(i * 2, 2)] = tile.reshape(2, 8, 3, 8, 1536).astype(BF)
        return carry

    lax.fori_loop(0, 4, outer, 0)

    def e_copy(h):
        there = pl.ds(pl.multiple_of(h * 768 + (1 - c) * 384, 384), 384)
        return remote(
            part.at[:, :, :, :, there], sib.at[h], e_s.at[h], e_r.at[h], sibling
        )

    for h in range(2):
        e_copy(h).start()
    for i in range(8):
        w_copy(i).wait_recv()

    def shape_w(i, carry):
        mat_w[pl.ds(pl.multiple_of(i * 192, 192), 192), :] = (
            weight[i].astype(F32).reshape(192, 1536).astype(BF)
        )
        return carry

    lax.fori_loop(0, 8, shape_w, 0)

    def forward(j, carry):
        span = pl.ds(pl.multiple_of(j * 256, 256), 256)
        tile = lax.dot_general(
            mat_h[...], mat_w[span, :], (((1,), (1,)), ((), ())), preferred_element_type=F32
        )
        out_send[:, :, span] = tile.reshape(80, 8, 256).astype(BF)
        return carry

    lax.fori_loop(0, 6, forward, 0)
    each(lambda k: o_copy(k).start())
    home_out[own] = out_send[own]

    def backward(j, carry):
        span = pl.ds(pl.multiple_of(j * 256, 256), 256)
        tile = jnp.dot(mat_g[...], mat_w[:, span], preferred_element_type=F32)
        back_send[:, :, span] = tile.reshape(80, 8, 256).astype(BF)
        return carry

    lax.fori_loop(0, 6, backward, 0)
    each(lambda k: b_copy(k).start())
    home_back[own] = back_send[own]

    for h in range(2):
        e_copy(h).wait_recv()

    def local(h, b):
        here = pl.ds(pl.multiple_of(h * 768 + c * 384, 384), 384)
        return part[:, b, :, :, here].astype(F32) + sib[h, :, b].astype(F32)

    def ring(h, s):
        if h == 0:
            return remote(
                ring_send.at[0, s], ring_recv.at[0, s], rp_s.at[s], rp_r.at[s], {"z": up}
            )
        return remote(
            ring_send.at[1, s], ring_recv.at[1, s], rm_s.at[s], rm_r.at[s], {"z": down}
        )

    for s in range(7):
        for h in range(2):
            b = lax.rem(z + 15 - s, 8) if h == 0 else lax.rem(z + 1 + s, 8)
            total = local(h, b)
            if s > 0:
                ring(h, s - 1).wait_recv()
                total = total + ring_recv[h, s - 1].astype(F32)
            ring_send[h, s] = total.astype(BF)
            ring(h, s).start()
    for h in range(2):
        total = local(h, z)
        ring(h, 6).wait_recv()
        last[h] = total + ring_recv[h, 6].astype(F32)
    each(lambda k: l_copy(k).start())
    grad_out[me] = last[yh, xy]

    each(lambda k: a_copy(k).wait_send())
    each(lambda k: h_copy(k).wait_send())
    each(lambda k: g_copy(k).wait_send())
    for s in range(4):
        zp_copy(s).wait_send()
    for s in range(3):
        zm_copy(s).wait_send()
    for i in range(8):
        w_copy(i).wait_send()
    for h in range(2):
        e_copy(h).wait_send()
        for s in range(7):
            ring(h, s).wait_send()
    each(lambda k: o_copy(k).wait())
    each(lambda k: b_copy(k).wait())
    each(lambda k: l_copy(k).wait())


def exchange(wq, send_h, send_g):
    vmem = pl.BlockSpec(memory_space=pltpu.VMEM)
    dma = lambda n: pltpu.SemaphoreType.DMA((n,))
    rows = pltpu.VMEM((80, 8, 1536), BF)
    mat = pltpu.VMEM((640, 1536), BF)
    return pl.pallas_call(
        core_kernel,
        out_shape=(
            jax.ShapeDtypeStruct((80, 8, 1536), BF),
            jax.ShapeDtypeStruct((80, 8, 1536), BF),
            jax.ShapeDtypeStruct((16, 3, 8, 384), F32),
        ),
        in_specs=[vmem] * 3,
        out_specs=(vmem,) * 3,
        scratch_shapes=[
            pltpu.VMEM((8, 8, 3, 8, 1536), BF),
            rows, rows, mat, mat,
            pltpu.VMEM((1536, 1536), BF),
            rows, rows,
            pltpu.VMEM((8, 8, 3, 8, 1536), BF),
            pltpu.VMEM((2, 8, 8, 3, 8, 384), BF),
            pltpu.VMEM((2, 7, 8, 3, 8, 384), BF),
            pltpu.VMEM((2, 7, 8, 3, 8, 384), BF),
            pltpu.VMEM((2, 8, 3, 8, 384), F32),
            dma(16), dma(16), dma(16), dma(16), dma(16), dma(16),
            dma(4), dma(4), dma(3), dma(3), dma(8), dma(8),
            dma(16), dma(16), dma(16), dma(16), dma(2), dma(2),
            dma(7), dma(7), dma(7), dma(7), dma(16), dma(16),
        ],
        compiler_params=pltpu.CompilerParams(
            collective_id=0, has_side_effects=True, vmem_limit_bytes=64000000
        ),
        name="exchange",
    )(wq, send_h, send_g)


def reduce_kernel(table, total, first, mine, second, done, p_s, p_r, q_s, q_r, t_s, t_r):
    x, yl, z = lax.axis_index("x"), lax.axis_index("yl"), lax.axis_index("z")
    yh, c = lax.axis_index("yh"), lax.axis_index("c")
    y = yh * 2 + yl
    me = x * 4 + y
    zc = z * 2 + c

    def line(k):
        oz = lax.rem(z + k // 2, 8)
        oc = lax.rem(c + lax.rem(k, 2), 2)
        return {"z": oz, "c": oc}

    def spot(px, py):
        return (
            pl.ds(pl.multiple_of(8 * px, 8), 8),
            pl.ds(pl.multiple_of(768 * py, 768), 768),
        )

    def each(do):
        def step(k, carry):
            do(k)
            return carry

        lax.fori_loop(1, 16, step, 0)

    barrier = pltpu.get_barrier_semaphore()

    def greet(k):
        px, py = offset(k, x, y)
        pl.semaphore_signal(barrier, inc=1, device_id=plane_id(px, py), device_id_type=MESH)
        pl.semaphore_signal(barrier, inc=1, device_id=line(k), device_id_type=MESH)

    each(greet)
    pl.semaphore_wait(barrier, 30)

    def p_copy(k):
        px, py = offset(k, x, y)
        return remote(
            table.at[spot(px, py)], first.at[me], p_s.at[k], p_r.at[k], plane_id(px, py)
        )

    def q_copy(k):
        return remote(mine, second.at[zc], q_s.at[k], q_r.at[k], line(k))

    def t_copy(k):
        px, py = offset(k, x, y)
        return remote(
            done, total.at[spot(x, y)], t_s.at[k], t_r.at[k], plane_id(px, py)
        )

    each(lambda k: p_copy(k).start())
    first[me] = table[spot(x, y)]
    each(lambda k: p_copy(k).wait_recv())
    mine[...] = jnp.sum(first[...], axis=0)
    each(lambda k: q_copy(k).start())
    second[zc] = mine[...]
    each(lambda k: q_copy(k).wait_recv())
    done[...] = jnp.sum(second[...], axis=0)
    each(lambda k: t_copy(k).start())
    total[spot(x, y)] = done[...]
    each(lambda k: p_copy(k).wait_send())
    each(lambda k: q_copy(k).wait_send())
    each(lambda k: t_copy(k).wait())


def reduce_all(table):
    vmem = pl.BlockSpec(memory_space=pltpu.VMEM)
    dma = pltpu.SemaphoreType.DMA((16,))
    return pl.pallas_call(
        reduce_kernel,
        out_shape=jax.ShapeDtypeStruct((32, 3072), F32),
        in_specs=[vmem],
        out_specs=vmem,
        scratch_shapes=[
            pltpu.VMEM((16, 8, 768), F32),
            pltpu.VMEM((8, 768), F32),
            pltpu.VMEM((16, 8, 768), F32),
            pltpu.VMEM((8, 768), F32),
            dma, dma, dma, dma, dma, dma,
        ],
        compiler_params=pltpu.CompilerParams(collective_id=1, has_side_effects=True),
        name="reduce_all",
    )(table)


def on_device(
    tokens, router_w, router_b, hidden, teacher_idx, merge_map, merge_coef, source_w, out_grad
):
    tok, feat = tokens.shape[1], tokens.shape[2]
    top, ffw = teacher_idx.shape[2], hidden.shape[3]
    dw = out_grad.shape[2]
    experts = router_w.shape[1]
    groups = 16
    copies = 4
    cap = 10
    slots = tok * top
    rows = 64 * cap
    quarter = ffw // 4
    grad_scale = 1.0 / math.sqrt(tok * 256)
    c, yh = lax.axis_index("c"), lax.axis_index("yh")
    x = tokens.reshape(tok, feat)
    hid = hidden.reshape(slots, ffw)
    og = out_grad.reshape(tok, dw)
    logits = jnp.dot(x, router_w, preferred_element_type=jnp.float32) + router_b
    choice = teacher_idx.reshape(tok, top)
    pick = choice[:, :, None] == jnp.arange(experts, dtype=jnp.int32)
    pick_float = pick.astype(jnp.float32)
    chosen = jnp.sum(pick_float * logits[:, None, :], axis=2)
    raised = jnp.exp(chosen)
    gate = raised / jnp.sum(raised, axis=1, keepdims=True)
    merged_id = jnp.sum(jnp.where(pick, merge_map[None, None, :], 0), axis=2)
    lane = (merged_id * copies + (jnp.arange(tok, dtype=jnp.int32) % copies)[:, None]).reshape(-1)
    onehot = (lane[:, None] == jnp.arange(64, dtype=jnp.int32)[None, :]).astype(jnp.bfloat16)
    lower = (
        jnp.arange(slots)[:, None] > jnp.arange(slots)[None, :]
    ).astype(jnp.bfloat16)
    before = jnp.dot(lower, onehot, preferred_element_type=jnp.float32)
    rank = jnp.sum(before * onehot.astype(jnp.float32), axis=1).astype(jnp.int32)
    index = jnp.where(rank < cap, lane * cap + rank, rows)
    select = (index[None, :] == jnp.arange(rows, dtype=jnp.int32)[:, None]).astype(jnp.bfloat16)
    slot_grad = (gate[:, :, None] * og[:, None, :]).astype(jnp.bfloat16).reshape(slots, dw)
    send_h = jnp.dot(select, hid, preferred_element_type=jnp.float32).astype(jnp.bfloat16)
    send_g = jnp.dot(select, slot_grad, preferred_element_type=jnp.float32).astype(jnp.bfloat16)

    ids = jnp.arange(experts, dtype=jnp.int32)
    same = merge_map[:, None] == merge_map[None, :]
    second = jnp.any(same & (ids[:, None] > ids[None, :]), axis=1)
    member = merge_map[None, :] == jnp.arange(groups, dtype=jnp.int32)[:, None]
    first_id = jnp.sum(jnp.where(member & ~second[None, :], ids[None, :], 0), axis=1)
    second_id = jnp.sum(jnp.where(member & second[None, :], ids[None, :], 0), axis=1)
    mine = lax.dynamic_slice_in_dim(source_w, (c * 2 + yh) * quarter, quarter, 2)
    merged = (
        merge_coef[first_id][:, None, None] * mine[first_id].astype(jnp.float32)
        + merge_coef[second_id][:, None, None] * mine[second_id].astype(jnp.float32)
    ).astype(jnp.bfloat16)
    share = source_w.shape[1]

    home_out, home_back, merged_grad = exchange(
        merged.reshape(groups, 3, 8, quarter),
        send_h.reshape(80, 8, ffw),
        send_g.reshape(80, 8, dw),
    )
    home_out = home_out.reshape(rows, dw)
    home_back = home_back.reshape(rows, ffw)
    merged_grad = merged_grad.reshape(groups, share, quarter)

    spread = (
        index[:, None] == jnp.arange(rows, dtype=jnp.int32)[None, :]
    ).astype(jnp.bfloat16)
    slot_out = jnp.dot(spread, home_out, preferred_element_type=jnp.float32)
    slot_out = slot_out.reshape(tok, top, dw)
    hidden_grad = (
        jnp.dot(spread, home_back, preferred_element_type=jnp.float32)
        .astype(jnp.bfloat16)
        .reshape(1, tok, top, ffw)
    )
    mixed = jnp.sum(gate[:, :, None] * slot_out, axis=1).astype(jnp.bfloat16)
    score = jnp.sum(og[:, None, :].astype(jnp.float32) * slot_out, axis=2)
    chosen_grad = gate * (score - jnp.sum(gate * score, axis=1, keepdims=True))
    logit_grad = jnp.sum(pick_float * chosen_grad[:, :, None], axis=1)
    logit_half = logit_grad.astype(jnp.bfloat16)
    token_grad = lax.dot_general(
        logit_half, router_w, (((1,), (1,)), ((), ())), preferred_element_type=jnp.float32
    ).astype(jnp.bfloat16)
    part_w = lax.dot_general(
        logit_half, x, (((0,), (0,)), ((), ())), preferred_element_type=jnp.float32
    )
    part_b = jnp.sum(logit_grad, axis=0)
    source_grad = merged_grad[merge_map]
    mine_out = lax.dynamic_slice_in_dim(source_w, (yh * 2 + c) * quarter, quarter, 2)
    part_c = jnp.sum(source_grad * mine_out.astype(jnp.float32), axis=(1, 2))
    source_w_grad = source_grad * (merge_coef * grad_scale)[:, None, None]
    table = jnp.concatenate(
        [
            part_w,
            part_b[:, None],
            part_c[:, None],
            jnp.zeros((experts, 3072 - feat - 2), jnp.float32),
        ],
        axis=1,
    )
    total = reduce_all(table) * grad_scale
    return (
        mixed.reshape(1, tok, dw),
        hidden_grad,
        token_grad.reshape(1, tok, feat),
        total[:, :feat].T,
        total[:, feat],
        total[:, feat + 1],
        source_w_grad,
    )


def solution(mesh):
    fine = jax.sharding.Mesh(mesh.devices.reshape(4, 2, 8, 2, 2), ("x", "yl", "z", "yh", "c"))
    ctx, rep = ("x", "yl", "z"), ("yh", "c")
    in_specs = (
        P(rep, ctx, None),
        P(),
        P(),
        P(rep, ctx, None, None),
        P(rep, ctx, None),
        P(),
        P(),
        P(None, ctx, None),
        P(rep, ctx, None),
    )
    out_specs = (
        P(rep, ctx, None),
        P(rep, ctx, None, None),
        P(rep, ctx, None),
        P(),
        P(),
        P(),
        P(None, ctx, rep),
    )
    return jax.shard_map(
        on_device, mesh=fine, in_specs=in_specs, out_specs=out_specs, check_vma=False
    )
```

```python
import math

import jax
import jax.numpy as jnp
from jax import lax
from jax.experimental import pallas as pl
from jax.experimental.pallas import tpu as pltpu
from jax.sharding import PartitionSpec as P

MESH = pl.DeviceIdType.MESH
BF = jnp.bfloat16
F32 = jnp.float32
CAP = 10
TOP = 4
ROWS = 640
SLOTS = 512
TOK = 128
WIDE = 1536
EXPERTS = 32
FEAT = 2880


def offset(k, x, y):
    px = lax.rem(x + k // 4, 4)
    py = lax.rem(y + lax.rem(k, 4), 4)
    return px, py


def plane_id(px, py):
    return {"x": px, "yl": lax.rem(py, 2), "yh": py // 2}


def remote(src, dst, send, recv, where):
    return pltpu.make_async_remote_copy(
        src_ref=src, dst_ref=dst, send_sem=send, recv_sem=recv, device_id=where,
        device_id_type=MESH,
    )


def spot(px, py):
    return (
        pl.ds(pl.multiple_of(8 * px, 8), 8),
        pl.ds(pl.multiple_of(768 * py, 768), 768),
    )


def each(do):
    def step(k, carry):
        do(k)
        return carry

    lax.fori_loop(1, 16, step, 0)


def iota(shape, dim):
    return lax.broadcasted_iota(jnp.int32, shape, dim)


def group_sum(v, lane):
    n = v.shape[1]
    v = v + jnp.where(lane % 2 == 0, pltpu.roll(v, n - 1, 1), pltpu.roll(v, 1, 1))
    return v + jnp.where(lane % 4 < 2, pltpu.roll(v, n - 2, 1), pltpu.roll(v, 2, 1))


def exact(a, b, dims):
    return lax.dot_general(
        a, b, (dims, ((), ())), precision=lax.Precision.HIGHEST, preferred_element_type=F32
    )


def kernel(
    grad_scale,
    tokens, router_t, bias, hid, idx, map_row, og, map_s, coef_s, source,
    mixed, hidden_grad, token_grad, total, small, expert_grad,
    src_a, src_b, wq, sel, og_rows, gate_s, pick_s, send_h, send_g,
    weight, recv_h, recv_g, mat_h, mat_g, mat_w, home_out, home_back,
    part, sib, ring_send, ring_recv, last, got,
    table, first, mine, second, done, row_a, row_b, row_c, row_d,
    l_sem,
    a_s, a_r, h_s, h_r, g_s, g_r, zp_s, zp_r, zm_s, zm_r, w_s, w_r,
    o_s, o_r, b_s, b_r, e_s, e_r, rp_s, rp_r, rm_s, rm_r, l_s, l_r,
    p_s, p_r, q_s, q_r, t_s, t_r, u_s, u_r, v_s, v_r,
):
    x, yl, z = lax.axis_index("x"), lax.axis_index("yl"), lax.axis_index("z")
    yh, c = lax.axis_index("yh"), lax.axis_index("c")
    y = yh * 2 + yl
    me = x * 4 + y
    xy = x * 2 + yl
    zc = z * 2 + c
    up, down = lax.rem(z + 1, 8), lax.rem(z + 7, 8)
    sibling = {"c": 1 - c}

    def line(k):
        return {"z": lax.rem(z + k // 2, 8), "c": lax.rem(c + lax.rem(k, 2), 2)}

    quarter = pl.ds(pl.multiple_of((c * 2 + yh) * 384, 384), 384)
    owned = pl.ds(pl.multiple_of((yh * 2 + c) * 384, 384), 384)
    half = pl.ds(pl.multiple_of(c * 768, 768), 768)
    load_a = pltpu.make_async_copy(source.at[:, :, :, quarter], src_a, l_sem.at[0])
    load_b = pltpu.make_async_copy(source.at[:, :, :, owned], src_b, l_sem.at[1])
    load_a.start()

    barrier = pltpu.get_barrier_semaphore()

    def greet(k):
        px, py = offset(k, x, y)
        pl.semaphore_signal(barrier, inc=1, device_id=plane_id(px, py), device_id_type=MESH)
        pl.semaphore_signal(barrier, inc=1, device_id=line(k), device_id_type=MESH)

    each(greet)

    lane = iota((1, SLOTS), 1)
    token_of = (iota((SLOTS, TOK), 0) // TOP == iota((SLOTS, TOK), 1)).astype(F32)
    ids = lax.dot_general(
        idx[...].astype(F32).astype(BF), token_of.astype(BF), (((1,), (1,)), ((), ())),
        preferred_element_type=F32,
    )
    idx_row = jnp.sum(
        jnp.where(iota((TOP, SLOTS), 0) == lane % TOP, ids, 0.0), axis=0, keepdims=True
    ).astype(jnp.int32)
    pick = iota((EXPERTS, SLOTS), 0) == idx_row
    square = iota((EXPERTS, EXPERTS), 0) == iota((EXPERTS, EXPERTS), 1)
    map_col = jnp.sum(
        jnp.where(square, map_row[...].astype(F32), 0.0), axis=1, keepdims=True
    )
    merged_row = jnp.sum(
        jnp.where(pick, map_col, 0.0), axis=0, keepdims=True
    ).astype(jnp.int32)
    lane_row = merged_row * 4 + (lane // TOP) % 4
    spread = iota((64, SLOTS), 0) == lane_row
    earlier = (iota((SLOTS, SLOTS), 0) < iota((SLOTS, SLOTS), 1)).astype(F32).astype(BF)
    before = jnp.dot(spread.astype(F32).astype(BF), earlier, preferred_element_type=F32)
    rank = jnp.sum(jnp.where(spread, before, 0.0), axis=0, keepdims=True).astype(jnp.int32)
    index_row = jnp.where(rank < CAP, lane_row * CAP + rank, ROWS)
    sel[...] = (iota((ROWS, SLOTS), 0) == index_row).astype(F32).astype(BF)
    pick_s[...] = pick.astype(F32)

    def pack_h(j, carry):
        span = pl.ds(pl.multiple_of(j * 256, 256), 256)
        tile = jnp.dot(sel[...], hid[:, span], preferred_element_type=F32)
        send_h[:, :, span] = tile.reshape(80, 8, 256).astype(BF)
        return carry

    lax.fori_loop(0, 6, pack_h, 0)

    load_a.wait()
    load_b.start()

    def merge(g, carry):
        one, two = jnp.int32(0), jnp.int32(0)
        for e in range(EXPERTS):
            two = jnp.where(map_s[e] == g, e, two)
        for e in reversed(range(EXPERTS)):
            one = jnp.where(map_s[e] == g, e, one)
        wq[g] = (
            coef_s[one] * src_a[one].astype(F32) + coef_s[two] * src_a[two].astype(F32)
        ).astype(BF)
        return carry

    lax.fori_loop(0, 16, merge, 0)
    pl.semaphore_wait(barrier, 30)

    def plane_copy(k, src, dst, send, recv):
        px, py = offset(k, x, y)
        return remote(
            src.at[pl.ds(5 * (px * 4 + py), 5)], dst.at[pl.ds(5 * me, 5)],
            send.at[k], recv.at[k], plane_id(px, py),
        )

    def a_copy(k):
        px, py = offset(k, x, y)
        return remote(
            wq.at[px * 4 + py], weight.at[xy, z, :, :, quarter], a_s.at[k], a_r.at[k],
            plane_id(px, py),
        )

    def h_copy(k):
        return plane_copy(k, send_h, recv_h, h_s, h_r)

    def g_copy(k):
        return plane_copy(k, send_g, recv_g, g_s, g_r)

    def o_copy(k):
        return plane_copy(k, send_h, home_out, o_s, o_r)

    def b_copy(k, n):
        px, py = offset(k, x, y)
        cols = pl.ds(n * 768, 768)
        return remote(
            send_g.at[pl.ds(5 * (px * 4 + py), 5), :, cols],
            home_back.at[pl.ds(5 * me, 5), :, cols],
            b_s.at[n, k], b_r.at[n, k], plane_id(px, py),
        )

    def l_copy(k):
        px, py = offset(k, x, y)
        return remote(
            last.at[py // 2, px * 2 + lax.rem(py, 2)], got.at[me],
            l_s.at[k], l_r.at[k], plane_id(px, py),
        )

    each(lambda k: a_copy(k).start())
    each(lambda k: h_copy(k).start())
    own = pl.ds(5 * me, 5)
    weight[xy, z, :, :, quarter] = wq[me]
    recv_h[own] = send_h[own]

    logits = jnp.dot(
        router_t[...], tokens[...], preferred_element_type=F32
    ) + jnp.sum(jnp.where(square, bias[...], 0.0), axis=1, keepdims=True)
    wide = exact(logits, token_of, ((1,), (1,)))
    chosen = jnp.sum(jnp.where(pick, wide, 0.0), axis=0, keepdims=True)
    raised = jnp.exp(chosen)
    gate = raised / group_sum(raised, lane)
    gate_s[...] = gate
    gate_col = jnp.sum(jnp.where(sel[...] > 0, gate, 0.0), axis=1, keepdims=True)
    row_token = jnp.dot(sel[...], token_of.astype(BF), preferred_element_type=F32).astype(BF)
    for j in range(6):
        span = pl.ds(j * 256, 256)
        tile = jnp.dot(row_token, og[:, span], preferred_element_type=F32)
        og_rows[:, span] = tile.astype(BF)
        send_g[:, :, span] = (tile * gate_col).reshape(80, 8, 256).astype(BF)
    each(lambda k: g_copy(k).start())
    recv_g[own] = send_g[own]

    each(lambda k: a_copy(k).wait_recv())

    def block(b):
        return weight.at[:, b, :, :, half]

    def w_copy(i):
        b = lax.rem(z + 8 - i, 8) if i <= 4 else lax.rem(z + i - 4, 8)
        return remote(block(b), block(b), w_s.at[i], w_r.at[i], sibling)

    def zp_copy(s):
        b = lax.rem(z + 8 - s, 8)
        return remote(block(b), block(b), zp_s.at[s], zp_r.at[s], {"z": up})

    def zm_copy(s):
        b = lax.rem(z + s, 8)
        return remote(block(b), block(b), zm_s.at[s], zm_r.at[s], {"z": down})

    zp_copy(0).start()
    zm_copy(0).start()
    w_copy(0).start()
    for s in range(4):
        zp_copy(s).wait_recv()
        if s < 3:
            zp_copy(s + 1).start()
        w_copy(s + 1).start()
        if s < 3:
            zm_copy(s).wait_recv()
            if s < 2:
                zm_copy(s + 1).start()
            w_copy(s + 5).start()

    def reshape_rows(src, dst):
        def step(i, carry):
            dst[pl.ds(pl.multiple_of(i * 80, 80), 80), :] = (
                src[pl.ds(i * 10, 10)].astype(F32).reshape(80, WIDE).astype(BF)
            )
            return carry

        lax.fori_loop(0, 8, step, 0)

    each(lambda k: h_copy(k).wait_recv())
    reshape_rows(recv_h, mat_h)
    for i in range(8):
        w_copy(i).wait_recv()

    def shape_w(i, carry):
        mat_w[pl.ds(pl.multiple_of(i * 192, 192), 192), :] = (
            weight[i].astype(F32).reshape(192, WIDE).astype(BF)
        )
        return carry

    lax.fori_loop(0, 8, shape_w, 0)
    each(lambda k: h_copy(k).wait_send())

    def forward(j, carry):
        span = pl.ds(pl.multiple_of(j * 256, 256), 256)
        tile = lax.dot_general(
            mat_h[...], mat_w[span, :], (((1,), (1,)), ((), ())), preferred_element_type=F32
        )
        send_h[:, :, span] = tile.reshape(80, 8, 256).astype(BF)
        return carry

    lax.fori_loop(0, 6, forward, 0)
    each(lambda k: o_copy(k).start())
    home_out[own] = send_h[own]
    each(lambda k: g_copy(k).wait_recv())
    reshape_rows(recv_g, mat_g)

    def outer(i, carry):
        cols = pl.ds(pl.multiple_of(i * 384, 384), 384)
        tile = lax.dot_general(
            mat_g[:, cols], mat_h[...], (((0,), (0,)), ((), ())), preferred_element_type=F32
        )
        part[pl.ds(i * 2, 2)] = tile.reshape(2, 8, 3, 8, WIDE).astype(BF)
        return carry

    lax.fori_loop(0, 4, outer, 0)

    def e_copy(h):
        there = pl.ds(pl.multiple_of(h * 768 + (1 - c) * 384, 384), 384)
        return remote(
            part.at[:, :, :, :, there], sib.at[h], e_s.at[h], e_r.at[h], sibling
        )

    for h in range(2):
        e_copy(h).start()
    each(lambda k: g_copy(k).wait_send())

    def backward(j, carry):
        span = pl.ds(pl.multiple_of(j * 256, 256), 256)
        tile = jnp.dot(mat_g[...], mat_w[:, span], preferred_element_type=F32)
        send_g[:, :, span] = tile.reshape(80, 8, 256).astype(BF)
        return carry

    def local(h, b):
        here = pl.ds(pl.multiple_of(h * 768 + c * 384, 384), 384)
        return part[:, b, :, :, here].astype(F32) + sib[h, :, b].astype(F32)

    def ring(h, s):
        if h == 0:
            return remote(
                ring_send.at[0, s], ring_recv.at[0, s], rp_s.at[s], rp_r.at[s], {"z": up}
            )
        return remote(
            ring_send.at[1, s], ring_recv.at[1, s], rm_s.at[s], rm_r.at[s], {"z": down}
        )

    def ring_step(s):
        for h in range(2):
            b = lax.rem(z + 15 - s, 8) if h == 0 else lax.rem(z + 1 + s, 8)
            value = local(h, b)
            if s > 0:
                ring(h, s - 1).wait_recv()
                value = value + ring_recv[h, s - 1].astype(F32)
            ring_send[h, s] = value.astype(BF)
            ring(h, s).start()

    lax.fori_loop(0, 3, backward, 0)
    each(lambda k: b_copy(k, 0).start())
    for h in range(2):
        e_copy(h).wait_recv()
    ring_step(0)
    lax.fori_loop(3, 6, backward, 0)
    each(lambda k: b_copy(k, 1).start())
    home_back[own] = send_g[own]
    for s in range(1, 7):
        ring_step(s)
    load_b.wait()
    for h in range(2):
        value = local(h, z)
        ring(h, 6).wait_recv()
        last[h] = (value + ring_recv[h, 6].astype(F32)).astype(BF)
    each(lambda k: l_copy(k).start())
    got[me] = last[yh, xy]

    each(lambda k: o_copy(k).wait_recv())

    def score_rows(i, carry):
        rows = pl.ds(pl.multiple_of(i * 80, 80), 80)
        value = home_out[pl.ds(i * 10, 10)].astype(F32).reshape(80, WIDE)
        mat_h[rows, :] = value.astype(BF)
        score = jnp.sum(value * og_rows[rows, :].astype(F32), axis=1, keepdims=True)
        return carry + jnp.sum(
            jnp.where(sel[rows, :] > 0, score, 0.0), axis=0, keepdims=True
        )

    score_row = lax.fori_loop(0, 8, score_rows, jnp.zeros((1, SLOTS), F32))
    gate = gate_s[...]
    chosen_grad = gate * (score_row - group_sum(gate * score_row, lane))
    slot_table = jnp.where(pick_s[...] > 0, chosen_grad, 0.0)
    logit_grad = exact(slot_table, token_of, ((1,), (0,)))
    logit_half = logit_grad.astype(BF)
    bias_col = jnp.sum(logit_grad, axis=1, keepdims=True)
    table[:, pl.ds(2816, 256)] = jnp.zeros((EXPERTS, 256), F32)
    table[:, pl.ds(0, FEAT)] = lax.dot_general(
        logit_half, tokens[...], (((1,), (1,)), ((), ())), preferred_element_type=F32
    )

    def p_copy(k):
        px, py = offset(k, x, y)
        return remote(
            table.at[spot(px, py)], first.at[me], p_s.at[k], p_r.at[k], plane_id(px, py)
        )

    def q_copy(k):
        return remote(mine, second.at[zc], q_s.at[k], q_r.at[k], line(k))

    def t_copy(k):
        px, py = offset(k, x, y)
        return remote(
            done, total.at[spot(x, y)], t_s.at[k], t_r.at[k], plane_id(px, py)
        )

    each(lambda k: p_copy(k).start())
    first[me] = table[spot(x, y)]
    each(lambda k: l_copy(k).wait_recv())

    def coefficient(e, carry):
        grad = got[map_s[e]].astype(F32)
        prod = jnp.sum(jnp.sum(grad * src_b[e].astype(F32), axis=0), axis=0, keepdims=True)
        dot = jnp.sum(prod, axis=1, keepdims=True)
        return carry + jnp.where(iota((1, 128), 1) == e, dot, 0.0)

    coef_row = lax.fori_loop(0, EXPERTS, coefficient, jnp.zeros((1, 128), F32))
    bias_row = jnp.sum(
        jnp.where(iota((EXPERTS, 128), 1) - 32 == iota((EXPERTS, 128), 0), bias_col, 0.0),
        axis=0, keepdims=True,
    )
    row_a[...] = jnp.broadcast_to(coef_row + bias_row, (8, 128))

    def u_copy(k):
        px, py = offset(k, x, y)
        return remote(row_a, row_b.at[me], u_s.at[k], u_r.at[k], plane_id(px, py))

    def v_copy(k):
        return remote(row_c, row_d.at[zc], v_s.at[k], v_r.at[k], line(k))

    each(lambda k: u_copy(k).start())
    row_b[me] = row_a[...]

    each(lambda k: p_copy(k).wait_recv())
    mine[...] = jnp.sum(first[...], axis=0)
    each(lambda k: q_copy(k).start())
    second[zc] = mine[...]

    def expert(e, carry):
        expert_grad[e] = got[map_s[e]].astype(F32) * (coef_s[e] * grad_scale)
        return carry

    lax.fori_loop(0, EXPERTS, expert, 0)
    each(lambda k: u_copy(k).wait_recv())
    row_c[...] = jnp.sum(row_b[...], axis=0)
    each(lambda k: v_copy(k).start())
    row_d[zc] = row_c[...]
    token_grad[...] = lax.dot_general(
        router_t[...], logit_half, (((0,), (0,)), ((), ())), preferred_element_type=F32
    ).astype(BF)
    each(lambda k: q_copy(k).wait_recv())
    done[...] = jnp.sum(second[...], axis=0) * grad_scale
    each(lambda k: t_copy(k).start())
    total[spot(x, y)] = done[...]
    slot_token = iota((TOK, SLOTS), 1) // TOP == iota((TOK, SLOTS), 0)
    spread_gate = jnp.where(slot_token, gate, 0.0)
    high = spread_gate.astype(BF)
    low = (spread_gate - high.astype(F32)).astype(BF)

    def over_rows(v):
        return lax.dot_general(
            v, sel[...], (((1,), (1,)), ((), ())), preferred_element_type=F32
        ).astype(BF)

    mixed[...] = (
        jnp.dot(over_rows(high), mat_h[...], preferred_element_type=F32)
        + jnp.dot(over_rows(low), mat_h[...], preferred_element_type=F32)
    ).astype(BF)
    for n in range(2):
        each(lambda k: b_copy(k, n).wait_recv())
    reshape_rows(home_back, mat_g)
    for j in range(6):
        span = pl.ds(j * 256, 256)
        hidden_grad[:, span] = lax.dot_general(
            sel[...], mat_g[:, span], (((0,), (0,)), ((), ())), preferred_element_type=F32
        ).astype(BF)
    each(lambda k: v_copy(k).wait_recv())
    small[...] = jnp.sum(row_d[...], axis=0) * grad_scale
    each(lambda k: t_copy(k).wait_recv())

    each(lambda k: a_copy(k).wait_send())
    for s in range(4):
        zp_copy(s).wait_send()
    for s in range(3):
        zm_copy(s).wait_send()
    for i in range(8):
        w_copy(i).wait_send()
    for h in range(2):
        e_copy(h).wait_send()
        for s in range(7):
            ring(h, s).wait_send()
    each(lambda k: o_copy(k).wait_send())
    for n in range(2):
        each(lambda k: b_copy(k, n).wait_send())
    each(lambda k: l_copy(k).wait_send())
    each(lambda k: p_copy(k).wait_send())
    each(lambda k: q_copy(k).wait_send())
    each(lambda k: t_copy(k).wait_send())
    each(lambda k: u_copy(k).wait_send())
    each(lambda k: v_copy(k).wait_send())


def on_device(
    tokens, router_w, router_b, hidden, teacher_idx, merge_map, merge_coef, source_w, out_grad
):
    grad_scale = 1.0 / math.sqrt(TOK * 256)
    vmem = pl.BlockSpec(memory_space=pltpu.VMEM)
    smem = pl.BlockSpec(memory_space=pltpu.SMEM)
    dma = lambda n: pltpu.SemaphoreType.DMA((n,))
    rows = pltpu.VMEM((80, 8, WIDE), BF)
    mat = pltpu.VMEM((ROWS, WIDE), BF)
    share = source_w.shape[1]

    def body(*refs):
        kernel(grad_scale, *refs)

    mixed, hidden_grad, token_grad, total, small, expert_grad = pl.pallas_call(
        body,
        out_shape=(
            jax.ShapeDtypeStruct((TOK, WIDE), BF),
            jax.ShapeDtypeStruct((SLOTS, WIDE), BF),
            jax.ShapeDtypeStruct((FEAT, TOK), BF),
            jax.ShapeDtypeStruct((EXPERTS, 3072), F32),
            jax.ShapeDtypeStruct((8, 128), F32),
            jax.ShapeDtypeStruct((EXPERTS, 3, 8, 384), F32),
        ),
        in_specs=[vmem] * 7 + [smem] * 2 + [pl.BlockSpec(memory_space=pl.ANY)],
        out_specs=(vmem,) * 6,
        scratch_shapes=[
            pltpu.VMEM((EXPERTS, 3, 8, 384), BF),
            pltpu.VMEM((EXPERTS, 3, 8, 384), BF),
            pltpu.VMEM((16, 3, 8, 384), BF),
            pltpu.VMEM((ROWS, SLOTS), BF),
            mat,
            pltpu.VMEM((1, SLOTS), F32),
            pltpu.VMEM((EXPERTS, SLOTS), F32),
            rows, rows,
            pltpu.VMEM((8, 8, 3, 8, WIDE), BF),
            rows, rows, mat, mat,
            pltpu.VMEM((WIDE, WIDE), BF),
            rows, rows,
            pltpu.VMEM((8, 8, 3, 8, WIDE), BF),
            pltpu.VMEM((2, 8, 8, 3, 8, 384), BF),
            pltpu.VMEM((2, 7, 8, 3, 8, 384), BF),
            pltpu.VMEM((2, 7, 8, 3, 8, 384), BF),
            pltpu.VMEM((2, 8, 3, 8, 384), BF),
            pltpu.VMEM((16, 3, 8, 384), BF),
            pltpu.VMEM((EXPERTS, 3072), F32),
            pltpu.VMEM((16, 8, 768), F32),
            pltpu.VMEM((8, 768), F32),
            pltpu.VMEM((16, 8, 768), F32),
            pltpu.VMEM((8, 768), F32),
            pltpu.VMEM((8, 128), F32),
            pltpu.VMEM((16, 8, 128), F32),
            pltpu.VMEM((8, 128), F32),
            pltpu.VMEM((16, 8, 128), F32),
            dma(2),
            dma(16), dma(16), dma(16), dma(16), dma(16), dma(16),
            dma(4), dma(4), dma(3), dma(3), dma(8), dma(8),
            dma(16), dma(16), pltpu.SemaphoreType.DMA((2, 16)), pltpu.SemaphoreType.DMA((2, 16)),
            dma(2), dma(2),
            dma(7), dma(7), dma(7), dma(7), dma(16), dma(16),
            dma(16), dma(16), dma(16), dma(16), dma(16), dma(16),
            dma(16), dma(16), dma(16), dma(16),
        ],
        compiler_params=pltpu.CompilerParams(
            collective_id=0, has_side_effects=True, vmem_limit_bytes=67043328
        ),
        name="whole",
    )(
        tokens[0].T,
        router_w.T,
        router_b.reshape(1, EXPERTS),
        hidden.reshape(SLOTS, WIDE),
        teacher_idx[0].T,
        merge_map.reshape(1, EXPERTS),
        out_grad.reshape(TOK, WIDE),
        merge_map,
        merge_coef,
        source_w.reshape(EXPERTS, 3, 8, WIDE),
    )
    return (
        mixed.reshape(1, TOK, WIDE),
        hidden_grad.reshape(1, TOK, TOP, WIDE),
        token_grad.T[None],
        total[:, :FEAT].T,
        small[0, 32:64],
        small[0, :32],
        expert_grad.reshape(EXPERTS, share, 384),
    )


def solution(mesh):
    fine = jax.sharding.Mesh(mesh.devices.reshape(4, 2, 8, 2, 2), ("x", "yl", "z", "yh", "c"))
    ctx, rep = ("x", "yl", "z"), ("yh", "c")
    in_specs = (
        P(rep, ctx, None),
        P(),
        P(),
        P(rep, ctx, None, None),
        P(rep, ctx, None),
        P(),
        P(),
        P(None, ctx, None),
        P(rep, ctx, None),
    )
    out_specs = (
        P(rep, ctx, None),
        P(rep, ctx, None, None),
        P(rep, ctx, None),
        P(),
        P(),
        P(),
        P(None, ctx, rep),
    )
    return jax.shard_map(
        on_device, mesh=fine, in_specs=in_specs, out_specs=out_specs, check_vma=False
    )
```

```python
import math

import jax
import jax.numpy as jnp
from jax import lax
from jax.experimental import pallas as pl
from jax.experimental.pallas import tpu as pltpu
from jax.sharding import PartitionSpec as P

MESH = pl.DeviceIdType.MESH
BF = jnp.bfloat16
F32 = jnp.float32
CAP = 10
TOP = 4
ROWS = 640
SLOTS = 512
TOK = 128
WIDE = 1536
EXPERTS = 32
FEAT = 2880


def offset(k, x, y):
    px = lax.rem(x + k // 4, 4)
    py = lax.rem(y + lax.rem(k, 4), 4)
    return px, py


def plane_id(px, py):
    return {"x": px, "yl": lax.rem(py, 2), "yh": py // 2}


def remote(src, dst, send, recv, where):
    return pltpu.make_async_remote_copy(
        src_ref=src, dst_ref=dst, send_sem=send, recv_sem=recv, device_id=where,
        device_id_type=MESH,
    )


def spot(px, py):
    return (
        pl.ds(pl.multiple_of(8 * px, 8), 8),
        pl.ds(pl.multiple_of(768 * py, 768), 768),
    )


def each(do):
    def step(k, carry):
        do(k)
        return carry

    lax.fori_loop(1, 16, step, 0)


def iota(shape, dim):
    return lax.broadcasted_iota(jnp.int32, shape, dim)


def group_sum(v, lane):
    n = v.shape[1]
    v = v + jnp.where(lane % 2 == 0, pltpu.roll(v, n - 1, 1), pltpu.roll(v, 1, 1))
    return v + jnp.where(lane % 4 < 2, pltpu.roll(v, n - 2, 1), pltpu.roll(v, 2, 1))


def exact(a, b, dims):
    return lax.dot_general(
        a, b, (dims, ((), ())), precision=lax.Precision.HIGHEST, preferred_element_type=F32
    )


def kernel(
    grad_scale,
    tokens, router_t, bias, hid, idx, map_row, og, map_s, coef_s, source,
    mixed, hidden_grad, token_grad, total, small, expert_grad,
    src_a, src_b, wq, sel, og_rows, gate_s, pick_s, send_h, send_g,
    weight, recv_h, recv_g, mat_h, mat_g, mat_w, home_out, home_back,
    part, sib, ring_send, ring_recv, last, got,
    table, first, mine, second, done, row_a, row_b, row_c, row_d, prods,
    l_sem,
    a_s, a_r, zp_s, zp_r, zm_s, zm_r, w_s, w_r, e_s, e_r, rp_s, rp_r, rm_s, rm_r, l_s, l_r,
    p_s, p_r, q_s, q_r, t_s, t_r, u_s, u_r, v_s, v_r,
    relay_h, relay_g, relay_o, relay_b, *sems,
):
    sem_h, sem_g, sem_o, sem_b = sems[:4], sems[4:8], sems[8:12], sems[12:]
    x, yl, z = lax.axis_index("x"), lax.axis_index("yl"), lax.axis_index("z")
    yh, c = lax.axis_index("yh"), lax.axis_index("c")
    y = yh * 2 + yl
    me = x * 4 + y
    xy = x * 2 + yl
    zc = z * 2 + c
    up, down = lax.rem(z + 1, 8), lax.rem(z + 7, 8)
    sibling = {"c": 1 - c}

    def line(k):
        return {"z": lax.rem(z + k // 2, 8), "c": lax.rem(c + lax.rem(k, 2), 2)}

    quarter = pl.ds(pl.multiple_of((c * 2 + yh) * 384, 384), 384)
    owned = pl.ds(pl.multiple_of((yh * 2 + c) * 384, 384), 384)
    half = pl.ds(pl.multiple_of(c * 768, 768), 768)
    load_a = pltpu.make_async_copy(source.at[:, :, :, quarter], src_a, l_sem.at[0])
    load_b = pltpu.make_async_copy(source.at[:, :, :, owned], src_b, l_sem.at[1])
    load_a.start()

    barrier = pltpu.get_barrier_semaphore()

    def greet(k):
        px, py = offset(k, x, y)
        pl.semaphore_signal(barrier, inc=1, device_id=plane_id(px, py), device_id_type=MESH)
        pl.semaphore_signal(barrier, inc=1, device_id=line(k), device_id_type=MESH)

    each(greet)

    lane = iota((1, SLOTS), 1)
    token_of = (iota((SLOTS, TOK), 0) // TOP == iota((SLOTS, TOK), 1)).astype(F32)
    ids = lax.dot_general(
        idx[...].astype(F32).astype(BF), token_of.astype(BF), (((1,), (1,)), ((), ())),
        preferred_element_type=F32,
    )
    idx_row = jnp.sum(
        jnp.where(iota((TOP, SLOTS), 0) == lane % TOP, ids, 0.0), axis=0, keepdims=True
    ).astype(jnp.int32)
    pick = iota((EXPERTS, SLOTS), 0) == idx_row
    square = iota((EXPERTS, EXPERTS), 0) == iota((EXPERTS, EXPERTS), 1)
    map_col = jnp.sum(
        jnp.where(square, map_row[...].astype(F32), 0.0), axis=1, keepdims=True
    )
    merged_row = jnp.sum(
        jnp.where(pick, map_col, 0.0), axis=0, keepdims=True
    ).astype(jnp.int32)
    lane_row = merged_row * 4 + (lane // TOP) % 4
    spread = iota((64, SLOTS), 0) == lane_row
    earlier = (iota((SLOTS, SLOTS), 0) < iota((SLOTS, SLOTS), 1)).astype(F32).astype(BF)
    before = jnp.dot(spread.astype(F32).astype(BF), earlier, preferred_element_type=F32)
    rank = jnp.sum(jnp.where(spread, before, 0.0), axis=0, keepdims=True).astype(jnp.int32)
    index_row = jnp.where(rank < CAP, lane_row * CAP + rank, ROWS)
    sel[...] = (iota((ROWS, SLOTS), 0) == index_row).astype(F32).astype(BF)
    pick_s[...] = pick.astype(F32)

    def slot_rows(i, carry):
        mat_g[pl.ds(pl.multiple_of(i * 64, 64), 64), :] = (
            hid[pl.ds(i * 16, 16)].astype(F32).reshape(64, WIDE).astype(BF)
        )
        return carry

    lax.fori_loop(0, 8, slot_rows, 0)

    def pack_h(j, carry):
        span = pl.ds(pl.multiple_of(j * 256, 256), 256)
        tile = jnp.dot(sel[...], mat_g[pl.ds(0, SLOTS), span], preferred_element_type=F32)
        send_h[:, :, :, :, span] = tile.reshape(4, 4, 5, 8, 256).astype(BF)
        return carry

    lax.fori_loop(0, 6, pack_h, 0)

    load_a.wait()
    load_b.start()

    def merge(g, carry):
        one, two = jnp.int32(0), jnp.int32(0)
        for e in range(EXPERTS):
            two = jnp.where(map_s[e] == g, e, two)
        for e in reversed(range(EXPERTS)):
            one = jnp.where(map_s[e] == g, e, one)
        wq[g] = (
            coef_s[one] * src_a[one].astype(F32) + coef_s[two] * src_a[two].astype(F32)
        ).astype(BF)
        return carry

    lax.fori_loop(0, 16, merge, 0)
    pl.semaphore_wait(barrier, 30)

    low_cols, high_cols = pl.ds(0, 768), pl.ds(768, 768)

    class Shuffle:
        def __init__(self, src, dst, relay, s1, r1, s2, r2):
            self.src, self.dst, self.relay = src, dst, relay
            self.s1, self.r1, self.s2, self.r2 = s1, r1, s2, r2

        def first(self, f, d):
            if f == 0:
                px = lax.rem(x + d, 4)
                src, where = self.src.at[px, :, :, :, low_cols], plane_id(px, y)
            else:
                py = lax.rem(y + d, 4)
                src, where = self.src.at[:, py, :, :, high_cols], plane_id(x, py)
            return remote(
                src, self.relay.at[f, d - 1], self.s1.at[f, d - 1], self.r1.at[f, d - 1], where
            )

        def second(self, f, d, e):
            if f == 0:
                py, px = lax.rem(y + e, 4), lax.rem(x + 4 - d, 4)
                src = (
                    self.src.at[x, py, :, :, low_cols] if d == 0 else self.relay.at[0, d - 1, py]
                )
                dst, where = self.dst.at[px, y, :, :, low_cols], plane_id(x, py)
            else:
                px, py = lax.rem(x + e, 4), lax.rem(y + 4 - d, 4)
                src = (
                    self.src.at[px, y, :, :, high_cols] if d == 0 else self.relay.at[1, d - 1, px]
                )
                dst, where = self.dst.at[x, py, :, :, high_cols], plane_id(px, y)
            return remote(src, dst, self.s2.at[f, d, e - 1], self.r2.at[f, d, e - 1], where)

        def start(self):
            for d in (1, 3, 2):
                for f in range(2):
                    self.first(f, d).start()
            for e in (1, 3, 2):
                for f in range(2):
                    self.second(f, 0, e).start()
            self.dst[x, y] = self.src[x, y]

        def forward(self, d):
            for f in range(2):
                self.first(f, d).wait_recv()
                for e in (1, 3, 2):
                    self.second(f, d, e).start()
            px, py = lax.rem(x + 4 - d, 4), lax.rem(y + 4 - d, 4)
            self.dst[px, y, :, :, low_cols] = self.relay[0, d - 1, y]
            self.dst[x, py, :, :, high_cols] = self.relay[1, d - 1, x]

        def arrive(self):
            for f in range(2):
                for d in range(4):
                    for e in range(1, 4):
                        self.second(f, d, e).wait_recv()

        def drain(self):
            for f in range(2):
                for d in range(1, 4):
                    self.first(f, d).wait_send()
                for d in range(4):
                    for e in range(1, 4):
                        self.second(f, d, e).wait_send()

    move_h = Shuffle(send_h, recv_h, relay_h, *sem_h)
    move_g = Shuffle(send_g, recv_g, relay_g, *sem_g)
    move_o = Shuffle(send_h, home_out, relay_o, *sem_o)
    move_b = Shuffle(send_g, home_back, relay_b, *sem_b)

    def a_copy(k):
        px, py = offset(k, x, y)
        return remote(
            wq.at[px * 4 + py], weight.at[xy, z, :, :, quarter], a_s.at[k], a_r.at[k],
            plane_id(px, py),
        )

    def l_copy(k):
        px, py = offset(k, x, y)
        return remote(
            last.at[py // 2, px * 2 + lax.rem(py, 2)], got.at[me],
            l_s.at[k], l_r.at[k], plane_id(px, py),
        )

    each(lambda k: a_copy(k).start())
    move_h.start()
    weight[xy, z, :, :, quarter] = wq[me]

    logits = jnp.dot(
        router_t[...], tokens[...], preferred_element_type=F32
    ) + jnp.sum(jnp.where(square, bias[...], 0.0), axis=1, keepdims=True)
    wide = exact(logits, token_of, ((1,), (1,)))
    chosen = jnp.sum(jnp.where(pick, wide, 0.0), axis=0, keepdims=True)
    raised = jnp.exp(chosen)
    gate = raised / group_sum(raised, lane)
    gate_s[...] = gate
    gate_col = jnp.sum(jnp.where(sel[...] > 0, gate, 0.0), axis=1, keepdims=True)
    row_token = jnp.dot(sel[...], token_of.astype(BF), preferred_element_type=F32).astype(BF)
    for j in range(6):
        span = pl.ds(j * 256, 256)
        tile = jnp.dot(row_token, og[:, span], preferred_element_type=F32)
        og_rows[:, span] = tile.astype(BF)
        send_g[:, :, :, :, span] = (tile * gate_col).reshape(4, 4, 5, 8, 256).astype(BF)
    move_g.start()

    each(lambda k: a_copy(k).wait_recv())

    def block(b):
        return weight.at[:, b, :, :, half]

    def w_copy(i):
        b = lax.rem(z + 8 - i, 8) if i <= 4 else lax.rem(z + i - 4, 8)
        return remote(block(b), block(b), w_s.at[i], w_r.at[i], sibling)

    def zp_copy(s):
        b = lax.rem(z + 8 - s, 8)
        return remote(block(b), block(b), zp_s.at[s], zp_r.at[s], {"z": up})

    def zm_copy(s):
        b = lax.rem(z + s, 8)
        return remote(block(b), block(b), zm_s.at[s], zm_r.at[s], {"z": down})

    zp_copy(0).start()
    zm_copy(0).start()
    w_copy(0).start()
    for s in range(4):
        if s == 0:
            move_h.forward(1)
            move_h.forward(3)
        elif s == 1:
            move_h.forward(2)
        elif s == 2:
            move_g.forward(1)
        else:
            move_g.forward(3)
        zp_copy(s).wait_recv()
        if s < 3:
            zp_copy(s + 1).start()
        w_copy(s + 1).start()
        if s < 3:
            zm_copy(s).wait_recv()
            if s < 2:
                zm_copy(s + 1).start()
            w_copy(s + 5).start()

    def reshape_rows(src, dst):
        def step(i, carry):
            dst[pl.ds(pl.multiple_of(i * 80, 80), 80), :] = (
                src[i // 2, pl.ds(lax.rem(i, 2) * 2, 2)].astype(F32).reshape(80, WIDE).astype(BF)
            )
            return carry

        lax.fori_loop(0, 8, step, 0)

    move_g.forward(2)
    move_h.arrive()
    reshape_rows(recv_h, mat_h)
    for i in range(8):
        w_copy(i).wait_recv()

    def shape_w(i, carry):
        mat_w[pl.ds(pl.multiple_of(i * 192, 192), 192), :] = (
            weight[i].astype(F32).reshape(192, WIDE).astype(BF)
        )
        return carry

    lax.fori_loop(0, 8, shape_w, 0)
    move_h.drain()

    def forward(j, carry):
        span = pl.ds(pl.multiple_of(j * 256, 256), 256)
        tile = lax.dot_general(
            mat_h[...], mat_w[span, :], (((1,), (1,)), ((), ())), preferred_element_type=F32
        )
        send_h[:, :, :, :, span] = tile.reshape(4, 4, 5, 8, 256).astype(BF)
        return carry

    lax.fori_loop(0, 6, forward, 0)
    move_o.start()
    move_g.arrive()
    reshape_rows(recv_g, mat_g)

    def outer(i, carry):
        cols = pl.ds(pl.multiple_of(i * 384, 384), 384)
        tile = lax.dot_general(
            mat_g[:, cols], mat_h[...], (((0,), (0,)), ((), ())), preferred_element_type=F32
        )
        part[pl.ds(i * 2, 2)] = tile.reshape(2, 8, 3, 8, WIDE).astype(BF)
        return carry

    lax.fori_loop(0, 4, outer, 0)

    def e_copy(h):
        there = pl.ds(pl.multiple_of(h * 768 + (1 - c) * 384, 384), 384)
        return remote(
            part.at[:, :, :, :, there], sib.at[h], e_s.at[h], e_r.at[h], sibling
        )

    for h in range(2):
        e_copy(h).start()
    move_g.drain()

    def backward(j, carry):
        span = pl.ds(pl.multiple_of(j * 256, 256), 256)
        tile = jnp.dot(mat_g[...], mat_w[:, span], preferred_element_type=F32)
        send_g[:, :, :, :, span] = tile.reshape(4, 4, 5, 8, 256).astype(BF)
        return carry

    def local(h, b):
        here = pl.ds(pl.multiple_of(h * 768 + c * 384, 384), 384)
        return part[:, b, :, :, here].astype(F32) + sib[h, :, b].astype(F32)

    def ring(h, s):
        if h == 0:
            return remote(
                ring_send.at[0, s], ring_recv.at[0, s], rp_s.at[s], rp_r.at[s], {"z": up}
            )
        return remote(
            ring_send.at[1, s], ring_recv.at[1, s], rm_s.at[s], rm_r.at[s], {"z": down}
        )

    def ring_step(s):
        for h in range(2):
            b = lax.rem(z + 15 - s, 8) if h == 0 else lax.rem(z + 1 + s, 8)
            value = local(h, b)
            if s > 0:
                ring(h, s - 1).wait_recv()
                value = value + ring_recv[h, s - 1].astype(F32)
            ring_send[h, s] = value.astype(BF)
            ring(h, s).start()

    move_o.forward(1)
    lax.fori_loop(0, 3, backward, 0)
    move_o.forward(3)
    lax.fori_loop(3, 6, backward, 0)
    move_b.start()
    for h in range(2):
        e_copy(h).wait_recv()
    ring_step(0)
    move_o.forward(2)
    ring_step(1)
    ring_step(2)
    move_b.forward(1)
    ring_step(3)
    move_b.forward(3)
    ring_step(4)
    move_b.forward(2)

    move_o.arrive()

    def score_rows(i, carry):
        rows = pl.ds(pl.multiple_of(i * 80, 80), 80)
        value = home_out[i // 2, pl.ds(lax.rem(i, 2) * 2, 2)].astype(F32).reshape(80, WIDE)
        mat_h[rows, :] = value.astype(BF)
        score = jnp.sum(value * og_rows[rows, :].astype(F32), axis=1, keepdims=True)
        return carry + jnp.sum(
            jnp.where(sel[rows, :] > 0, score, 0.0), axis=0, keepdims=True
        )

    score_row = lax.fori_loop(0, 8, score_rows, jnp.zeros((1, SLOTS), F32))
    gate = gate_s[...]
    chosen_grad = gate * (score_row - group_sum(gate * score_row, lane))
    slot_table = jnp.where(pick_s[...] > 0, chosen_grad, 0.0)
    logit_grad = exact(slot_table, token_of, ((1,), (0,)))
    logit_half = logit_grad.astype(BF)
    bias_col = jnp.sum(logit_grad, axis=1, keepdims=True)
    table[:, pl.ds(2816, 256)] = jnp.zeros((EXPERTS, 256), F32)
    table[:, pl.ds(0, FEAT)] = lax.dot_general(
        logit_half, tokens[...], (((1,), (1,)), ((), ())), preferred_element_type=F32
    )

    def p_copy(k):
        px, py = offset(k, x, y)
        return remote(
            table.at[spot(px, py)], first.at[me], p_s.at[k], p_r.at[k], plane_id(px, py)
        )

    def q_copy(k):
        return remote(mine, second.at[zc], q_s.at[k], q_r.at[k], line(k))

    def t_copy(k):
        px, py = offset(k, x, y)
        return remote(
            done, total.at[spot(x, y)], t_s.at[k], t_r.at[k], plane_id(px, py)
        )

    each(lambda k: p_copy(k).start())
    first[me] = table[spot(x, y)]
    for s in range(5, 7):
        ring_step(s)
    load_b.wait()
    for h in range(2):
        value = local(h, z)
        ring(h, 6).wait_recv()
        last[h] = (value + ring_recv[h, 6].astype(F32)).astype(BF)
    each(lambda k: l_copy(k).start())
    got[me] = last[yh, xy]

    each(lambda k: p_copy(k).wait_recv())
    mine[...] = jnp.sum(first[...], axis=0)
    each(lambda k: q_copy(k).start())
    second[zc] = mine[...]
    each(lambda k: l_copy(k).wait_recv())

    def coefficient(e, carry):
        prod = jnp.sum(got[map_s[e]].astype(F32) * src_b[e].astype(F32), axis=0)
        prods[e] = prod[:, :128] + prod[:, 128:256] + prod[:, 256:]
        return carry

    lax.fori_loop(0, EXPERTS, coefficient, 0)
    dots = jnp.sum(jnp.sum(prods[...], axis=1), axis=1, keepdims=True)
    at = iota((EXPERTS, 128), 1) == iota((EXPERTS, 128), 0)
    coef_row = jnp.sum(jnp.where(at, dots, 0.0), axis=0, keepdims=True)
    bias_row = jnp.sum(
        jnp.where(iota((EXPERTS, 128), 1) - 32 == iota((EXPERTS, 128), 0), bias_col, 0.0),
        axis=0, keepdims=True,
    )
    row_a[...] = jnp.broadcast_to(coef_row + bias_row, (8, 128))

    def u_copy(k):
        px, py = offset(k, x, y)
        return remote(row_a, row_b.at[me], u_s.at[k], u_r.at[k], plane_id(px, py))

    def v_copy(k):
        return remote(row_c, row_d.at[zc], v_s.at[k], v_r.at[k], line(k))

    each(lambda k: u_copy(k).start())
    row_b[me] = row_a[...]

    each(lambda k: q_copy(k).wait_recv())
    done[...] = jnp.sum(second[...], axis=0) * grad_scale
    each(lambda k: t_copy(k).start())
    total[spot(x, y)] = done[...]

    def expert(e, carry):
        expert_grad[e] = got[map_s[e]].astype(F32) * (coef_s[e] * grad_scale)
        return carry

    lax.fori_loop(0, EXPERTS, expert, 0)
    each(lambda k: u_copy(k).wait_recv())
    row_c[...] = jnp.sum(row_b[...], axis=0)
    each(lambda k: v_copy(k).start())
    row_d[zc] = row_c[...]
    token_grad[...] = lax.dot_general(
        router_t[...], logit_half, (((0,), (0,)), ((), ())), preferred_element_type=F32
    ).astype(BF)
    slot_token = iota((TOK, SLOTS), 1) // TOP == iota((TOK, SLOTS), 0)
    spread_gate = jnp.where(slot_token, gate, 0.0)
    high = spread_gate.astype(BF)
    low = (spread_gate - high.astype(F32)).astype(BF)

    def over_rows(v):
        return lax.dot_general(
            v, sel[...], (((1,), (1,)), ((), ())), preferred_element_type=F32
        ).astype(BF)

    mixed[...] = (
        jnp.dot(over_rows(high), mat_h[...], preferred_element_type=F32)
        + jnp.dot(over_rows(low), mat_h[...], preferred_element_type=F32)
    ).astype(BF)
    move_b.arrive()
    reshape_rows(home_back, mat_g)
    for j in range(6):
        span = pl.ds(j * 256, 256)
        tile = lax.dot_general(
            sel[...], mat_g[:, span], (((0,), (0,)), ((), ())), preferred_element_type=F32
        )
        hidden_grad[:, :, span] = tile.reshape(TOK, TOP, 256).astype(BF)
    each(lambda k: v_copy(k).wait_recv())
    small[...] = jnp.sum(row_d[...], axis=0) * grad_scale
    each(lambda k: t_copy(k).wait_recv())

    each(lambda k: a_copy(k).wait_send())
    for s in range(4):
        zp_copy(s).wait_send()
    for s in range(3):
        zm_copy(s).wait_send()
    for i in range(8):
        w_copy(i).wait_send()
    for h in range(2):
        e_copy(h).wait_send()
        for s in range(7):
            ring(h, s).wait_send()
    move_o.drain()
    move_b.drain()
    each(lambda k: l_copy(k).wait_send())
    each(lambda k: p_copy(k).wait_send())
    each(lambda k: q_copy(k).wait_send())
    each(lambda k: t_copy(k).wait_send())
    each(lambda k: u_copy(k).wait_send())
    each(lambda k: v_copy(k).wait_send())


def on_device(
    tokens, router_w, router_b, hidden, teacher_idx, merge_map, merge_coef, source_w, out_grad
):
    grad_scale = 1.0 / math.sqrt(TOK * 256)
    vmem = pl.BlockSpec(memory_space=pltpu.VMEM)
    smem = pl.BlockSpec(memory_space=pltpu.SMEM)
    dma = lambda n: pltpu.SemaphoreType.DMA((n,))
    rows = pltpu.VMEM((4, 4, 5, 8, WIDE), BF)
    relay = pltpu.VMEM((2, 3, 4, 5, 8, 768), BF)
    one = pltpu.SemaphoreType.DMA((2, 3))
    two = pltpu.SemaphoreType.DMA((2, 4, 3))
    mat = pltpu.VMEM((ROWS, WIDE), BF)
    share = source_w.shape[1]

    def body(*refs):
        kernel(grad_scale, *refs)

    mixed, hidden_grad, token_grad, total, small, expert_grad = pl.pallas_call(
        body,
        out_shape=(
            jax.ShapeDtypeStruct((TOK, WIDE), BF),
            jax.ShapeDtypeStruct((TOK, TOP, WIDE), BF),
            jax.ShapeDtypeStruct((FEAT, TOK), BF),
            jax.ShapeDtypeStruct((EXPERTS, 3072), F32),
            jax.ShapeDtypeStruct((8, 128), F32),
            jax.ShapeDtypeStruct((EXPERTS, 3, 8, 384), F32),
        ),
        in_specs=[vmem] * 7 + [smem] * 2 + [pl.BlockSpec(memory_space=pl.ANY)],
        out_specs=(vmem,) * 6,
        scratch_shapes=[
            pltpu.VMEM((EXPERTS, 3, 8, 384), BF),
            pltpu.VMEM((EXPERTS, 3, 8, 384), BF),
            pltpu.VMEM((16, 3, 8, 384), BF),
            pltpu.VMEM((ROWS, SLOTS), BF),
            mat,
            pltpu.VMEM((1, SLOTS), F32),
            pltpu.VMEM((EXPERTS, SLOTS), F32),
            rows, rows,
            pltpu.VMEM((8, 8, 3, 8, WIDE), BF),
            rows, rows, mat, mat,
            pltpu.VMEM((WIDE, WIDE), BF),
            rows, rows,
            pltpu.VMEM((8, 8, 3, 8, WIDE), BF),
            pltpu.VMEM((2, 8, 8, 3, 8, 384), BF),
            pltpu.VMEM((2, 7, 8, 3, 8, 384), BF),
            pltpu.VMEM((2, 7, 8, 3, 8, 384), BF),
            pltpu.VMEM((2, 8, 3, 8, 384), BF),
            pltpu.VMEM((16, 3, 8, 384), BF),
            pltpu.VMEM((EXPERTS, 3072), F32),
            pltpu.VMEM((16, 8, 768), F32),
            pltpu.VMEM((8, 768), F32),
            pltpu.VMEM((16, 8, 768), F32),
            pltpu.VMEM((8, 768), F32),
            pltpu.VMEM((8, 128), F32),
            pltpu.VMEM((16, 8, 128), F32),
            pltpu.VMEM((8, 128), F32),
            pltpu.VMEM((16, 8, 128), F32),
            pltpu.VMEM((EXPERTS, 8, 128), F32),
            dma(2),
            dma(16), dma(16), dma(4), dma(4), dma(3), dma(3), dma(8), dma(8),
            dma(2), dma(2),
            dma(7), dma(7), dma(7), dma(7), dma(16), dma(16),
            dma(16), dma(16), dma(16), dma(16), dma(16), dma(16),
            dma(16), dma(16), dma(16), dma(16),
            relay, relay, relay, relay,
        ]
        + [one, one, two, two] * 4,
        compiler_params=pltpu.CompilerParams(
            collective_id=0, has_side_effects=True, vmem_limit_bytes=67043328
        ),
        name="whole",
    )(
        tokens[0].T,
        router_w.T,
        router_b.reshape(1, EXPERTS),
        hidden[0],
        teacher_idx[0].T,
        merge_map.reshape(1, EXPERTS),
        out_grad.reshape(TOK, WIDE),
        merge_map,
        merge_coef,
        source_w.reshape(EXPERTS, 3, 8, WIDE),
    )
    return (
        mixed.reshape(1, TOK, WIDE),
        hidden_grad[None],
        token_grad.T[None],
        total[:, :FEAT].T,
        small[0, 32:64],
        small[0, :32],
        expert_grad.reshape(EXPERTS, share, 384),
    )


def solution(mesh):
    fine = jax.sharding.Mesh(mesh.devices.reshape(4, 2, 8, 2, 2), ("x", "yl", "z", "yh", "c"))
    ctx, rep = ("x", "yl", "z"), ("yh", "c")
    in_specs = (
        P(rep, ctx, None),
        P(),
        P(),
        P(rep, ctx, None, None),
        P(rep, ctx, None),
        P(),
        P(),
        P(None, ctx, None),
        P(rep, ctx, None),
    )
    out_specs = (
        P(rep, ctx, None),
        P(rep, ctx, None, None),
        P(rep, ctx, None),
        P(),
        P(),
        P(),
        P(None, ctx, rep),
    )
    return jax.shard_map(
        on_device, mesh=fine, in_specs=in_specs, out_specs=out_specs, check_vma=False
    )
```

```python
import math

import jax
import jax.numpy as jnp
from jax import lax
from jax.experimental import pallas as pl
from jax.experimental.pallas import tpu as pltpu
from jax.sharding import PartitionSpec as P

MESH = pl.DeviceIdType.MESH
BF = jnp.bfloat16
F32 = jnp.float32
CAP = 10
TOP = 4
ROWS = 640
SLOTS = 512
TOK = 128
WIDE = 1536
EXPERTS = 32
FEAT = 2880


def offset(k, x, y):
    px = lax.rem(x + k // 4, 4)
    py = lax.rem(y + lax.rem(k, 4), 4)
    return px, py


def plane_id(px, py):
    return {"x": px, "yl": lax.rem(py, 2), "yh": py // 2}


def remote(src, dst, send, recv, where):
    return pltpu.make_async_remote_copy(
        src_ref=src, dst_ref=dst, send_sem=send, recv_sem=recv, device_id=where,
        device_id_type=MESH,
    )


def spot(px, py):
    return (
        pl.ds(pl.multiple_of(8 * px, 8), 8),
        pl.ds(pl.multiple_of(768 * py, 768), 768),
    )


def each(do):
    def step(k, carry):
        do(k)
        return carry

    lax.fori_loop(1, 16, step, 0)


def iota(shape, dim):
    return lax.broadcasted_iota(jnp.int32, shape, dim)


def group_sum(v, lane):
    n = v.shape[1]
    v = v + jnp.where(lane % 2 == 0, pltpu.roll(v, n - 1, 1), pltpu.roll(v, 1, 1))
    return v + jnp.where(lane % 4 < 2, pltpu.roll(v, n - 2, 1), pltpu.roll(v, 2, 1))


def exact(a, b, dims):
    return lax.dot_general(
        a, b, (dims, ((), ())), precision=lax.Precision.HIGHEST, preferred_element_type=F32
    )


def kernel(
    grad_scale,
    tokens, router_t, bias, hid, idx, map_row, og, map_s, coef_s, source,
    mixed, hidden_grad, token_grad, total, small, expert_grad,
    src_a, src_b, wq, sel, og_rows, gate_s, pick_s, send_h, send_g,
    weight, recv_h, recv_g, mat_h, mat_g, mat_w, home_out, home_back,
    part, sib, ring_send, ring_recv, last, got,
    table, first, mine, second, done, row_a, row_b, row_c, row_d, prods,
    l_sem,
    a_s, a_r, zp_s, zp_r, zm_s, zm_r, w_s, w_r, e_s, e_r, rp_s, rp_r, rm_s, rm_r, l_s, l_r,
    p_s, p_r, q_s, q_r, t_s, t_r, u_s, u_r, v_s, v_r,
    relay_h, relay_g, relay_o, relay_b, *sems,
):
    sem_h, sem_g, sem_o, sem_b = sems[:4], sems[4:8], sems[8:12], sems[12:]
    x, yl, z = lax.axis_index("x"), lax.axis_index("yl"), lax.axis_index("z")
    yh, c = lax.axis_index("yh"), lax.axis_index("c")
    y = yh * 2 + yl
    me = x * 4 + y
    xy = x * 2 + yl
    zc = z * 2 + c
    up, down = lax.rem(z + 1, 8), lax.rem(z + 7, 8)
    sibling = {"c": 1 - c}

    def line(k):
        return {"z": lax.rem(z + k // 2, 8), "c": lax.rem(c + lax.rem(k, 2), 2)}

    quarter = pl.ds(pl.multiple_of((c * 2 + yh) * 384, 384), 384)
    owned = pl.ds(pl.multiple_of((yh * 2 + c) * 384, 384), 384)
    half = pl.ds(pl.multiple_of(c * 768, 768), 768)
    load_a = pltpu.make_async_copy(source.at[:, :, :, quarter], src_a, l_sem.at[0])
    load_b = pltpu.make_async_copy(source.at[:, :, :, owned], src_b, l_sem.at[1])
    load_a.start()

    barrier = pltpu.get_barrier_semaphore()

    def greet(k):
        px, py = offset(k, x, y)
        pl.semaphore_signal(barrier, inc=1, device_id=plane_id(px, py), device_id_type=MESH)
        pl.semaphore_signal(barrier, inc=1, device_id=line(k), device_id_type=MESH)

    each(greet)

    lane = iota((1, SLOTS), 1)
    token_of = (iota((SLOTS, TOK), 0) // TOP == iota((SLOTS, TOK), 1)).astype(F32)
    ids = lax.dot_general(
        idx[...].astype(F32).astype(BF), token_of.astype(BF), (((1,), (1,)), ((), ())),
        preferred_element_type=F32,
    )
    idx_row = jnp.sum(
        jnp.where(iota((TOP, SLOTS), 0) == lane % TOP, ids, 0.0), axis=0, keepdims=True
    ).astype(jnp.int32)
    pick = iota((EXPERTS, SLOTS), 0) == idx_row
    square = iota((EXPERTS, EXPERTS), 0) == iota((EXPERTS, EXPERTS), 1)
    map_col = jnp.sum(
        jnp.where(square, map_row[...].astype(F32), 0.0), axis=1, keepdims=True
    )
    merged_row = jnp.sum(
        jnp.where(pick, map_col, 0.0), axis=0, keepdims=True
    ).astype(jnp.int32)
    lane_row = merged_row * 4 + (lane // TOP) % 4
    spread = iota((64, SLOTS), 0) == lane_row
    earlier = (iota((SLOTS, SLOTS), 0) < iota((SLOTS, SLOTS), 1)).astype(F32).astype(BF)
    before = jnp.dot(spread.astype(F32).astype(BF), earlier, preferred_element_type=F32)
    rank = jnp.sum(jnp.where(spread, before, 0.0), axis=0, keepdims=True).astype(jnp.int32)
    index_row = jnp.where(rank < CAP, lane_row * CAP + rank, ROWS)
    sel[...] = (iota((ROWS, SLOTS), 0) == index_row).astype(F32).astype(BF)
    pick_s[...] = pick.astype(F32)

    def slot_rows(i, carry):
        mat_g[pl.ds(pl.multiple_of(i * 64, 64), 64), :] = (
            hid[pl.ds(i * 16, 16)].astype(F32).reshape(64, WIDE).astype(BF)
        )
        return carry

    lax.fori_loop(0, 8, slot_rows, 0)

    def pack_h(j, carry):
        span = pl.ds(pl.multiple_of(j * 256, 256), 256)
        tile = jnp.dot(sel[...], mat_g[pl.ds(0, SLOTS), span], preferred_element_type=F32)
        send_h[:, :, :, :, span] = tile.reshape(4, 4, 5, 8, 256).astype(BF)
        return carry

    lax.fori_loop(0, 6, pack_h, 0)

    load_a.wait()
    load_b.start()

    def merge(g, carry):
        one, two = jnp.int32(0), jnp.int32(0)
        for e in range(EXPERTS):
            two = jnp.where(map_s[e] == g, e, two)
        for e in reversed(range(EXPERTS)):
            one = jnp.where(map_s[e] == g, e, one)
        wq[g] = (
            coef_s[one] * src_a[one].astype(F32) + coef_s[two] * src_a[two].astype(F32)
        ).astype(BF)
        return carry

    lax.fori_loop(0, 16, merge, 0)
    pl.semaphore_wait(barrier, 30)

    low_cols, high_cols = pl.ds(0, 768), pl.ds(768, 768)

    class Shuffle:
        def __init__(self, src, dst, relay, s1, r1, s2, r2):
            self.src, self.dst, self.relay = src, dst, relay
            self.s1, self.r1, self.s2, self.r2 = s1, r1, s2, r2

        def first(self, f, d):
            if f == 0:
                px = lax.rem(x + d, 4)
                src, where = self.src.at[px, :, :, :, low_cols], plane_id(px, y)
            else:
                py = lax.rem(y + d, 4)
                src, where = self.src.at[:, py, :, :, high_cols], plane_id(x, py)
            return remote(
                src, self.relay.at[f, d - 1], self.s1.at[f, d - 1], self.r1.at[f, d - 1], where
            )

        def second(self, f, d, e):
            if f == 0:
                py, px = lax.rem(y + e, 4), lax.rem(x + 4 - d, 4)
                src = (
                    self.src.at[x, py, :, :, low_cols] if d == 0 else self.relay.at[0, d - 1, py]
                )
                dst, where = self.dst.at[px, y, :, :, low_cols], plane_id(x, py)
            else:
                px, py = lax.rem(x + e, 4), lax.rem(y + 4 - d, 4)
                src = (
                    self.src.at[px, y, :, :, high_cols] if d == 0 else self.relay.at[1, d - 1, px]
                )
                dst, where = self.dst.at[x, py, :, :, high_cols], plane_id(px, y)
            return remote(src, dst, self.s2.at[f, d, e - 1], self.r2.at[f, d, e - 1], where)

        def start(self):
            for d in (1, 3, 2):
                for f in range(2):
                    self.first(f, d).start()
            for e in (1, 3, 2):
                for f in range(2):
                    self.second(f, 0, e).start()
            self.dst[x, y] = self.src[x, y]

        def forward(self, d):
            for f in range(2):
                self.first(f, d).wait_recv()
                for e in (1, 3, 2):
                    self.second(f, d, e).start()
            px, py = lax.rem(x + 4 - d, 4), lax.rem(y + 4 - d, 4)
            self.dst[px, y, :, :, low_cols] = self.relay[0, d - 1, y]
            self.dst[x, py, :, :, high_cols] = self.relay[1, d - 1, x]

        def arrive(self):
            for f in range(2):
                for d in range(4):
                    for e in range(1, 4):
                        self.second(f, d, e).wait_recv()

        def drain(self):
            for f in range(2):
                for d in range(1, 4):
                    self.first(f, d).wait_send()
                for d in range(4):
                    for e in range(1, 4):
                        self.second(f, d, e).wait_send()

    move_h = Shuffle(send_h, recv_h, relay_h, *sem_h)
    move_g = Shuffle(send_g, recv_g, relay_g, *sem_g)
    move_o = Shuffle(send_h, home_out, relay_o, *sem_o)
    move_b = Shuffle(send_g, home_back, relay_b, *sem_b)

    def a_copy(k):
        px, py = offset(k, x, y)
        return remote(
            wq.at[px * 4 + py], weight.at[xy, z, :, :, quarter], a_s.at[k], a_r.at[k],
            plane_id(px, py),
        )

    def l_copy(k):
        px, py = offset(k, x, y)
        return remote(
            last.at[py // 2, px * 2 + lax.rem(py, 2)], got.at[me],
            l_s.at[k], l_r.at[k], plane_id(px, py),
        )

    each(lambda k: a_copy(k).start())
    move_h.start()
    weight[xy, z, :, :, quarter] = wq[me]

    logits = jnp.dot(
        router_t[...], tokens[...], preferred_element_type=F32
    ) + jnp.sum(jnp.where(square, bias[...], 0.0), axis=1, keepdims=True)
    wide = exact(logits, token_of, ((1,), (1,)))
    chosen = jnp.sum(jnp.where(pick, wide, 0.0), axis=0, keepdims=True)
    raised = jnp.exp(chosen)
    gate = raised / group_sum(raised, lane)
    gate_s[...] = gate
    gate_col = jnp.sum(jnp.where(sel[...] > 0, gate, 0.0), axis=1, keepdims=True)
    row_token = jnp.dot(sel[...], token_of.astype(BF), preferred_element_type=F32).astype(BF)
    for j in range(6):
        span = pl.ds(j * 256, 256)
        tile = jnp.dot(row_token, og[:, span], preferred_element_type=F32)
        og_rows[:, span] = tile.astype(BF)
        send_g[:, :, :, :, span] = (tile * gate_col).reshape(4, 4, 5, 8, 256).astype(BF)
    move_g.start()

    each(lambda k: a_copy(k).wait_recv())

    def block(b):
        return weight.at[:, b, :, :, half]

    def w_copy(i):
        b = lax.rem(z + 8 - i, 8) if i <= 4 else lax.rem(z + i - 4, 8)
        return remote(block(b), block(b), w_s.at[i], w_r.at[i], sibling)

    def zp_copy(s):
        b = lax.rem(z + 8 - s, 8)
        return remote(block(b), block(b), zp_s.at[s], zp_r.at[s], {"z": up})

    def zm_copy(s):
        b = lax.rem(z + s, 8)
        return remote(block(b), block(b), zm_s.at[s], zm_r.at[s], {"z": down})

    zp_copy(0).start()
    zm_copy(0).start()
    w_copy(0).start()
    for s in range(4):
        if s == 0:
            move_h.forward(1)
            move_h.forward(3)
        elif s == 1:
            move_h.forward(2)
        elif s == 2:
            move_g.forward(1)
        else:
            move_g.forward(3)
        zp_copy(s).wait_recv()
        if s < 3:
            zp_copy(s + 1).start()
        w_copy(s + 1).start()
        if s < 3:
            zm_copy(s).wait_recv()
            if s < 2:
                zm_copy(s + 1).start()
            w_copy(s + 5).start()

    def reshape_rows(src, dst):
        def step(i, carry):
            dst[pl.ds(pl.multiple_of(i * 80, 80), 80), :] = (
                src[i // 2, pl.ds(lax.rem(i, 2) * 2, 2)].astype(F32).reshape(80, WIDE).astype(BF)
            )
            return carry

        lax.fori_loop(0, 8, step, 0)

    move_g.forward(2)
    move_h.arrive()
    reshape_rows(recv_h, mat_h)
    for i in range(8):
        w_copy(i).wait_recv()

    def shape_w(i, carry):
        mat_w[pl.ds(pl.multiple_of(i * 192, 192), 192), :] = (
            weight[i].astype(F32).reshape(192, WIDE).astype(BF)
        )
        return carry

    lax.fori_loop(0, 8, shape_w, 0)
    move_h.drain()

    def forward(j, carry):
        span = pl.ds(pl.multiple_of(j * 256, 256), 256)
        tile = lax.dot_general(
            mat_h[...], mat_w[span, :], (((1,), (1,)), ((), ())), preferred_element_type=F32
        )
        send_h[:, :, :, :, span] = tile.reshape(4, 4, 5, 8, 256).astype(BF)
        return carry

    lax.fori_loop(0, 6, forward, 0)
    move_o.start()
    move_g.arrive()
    reshape_rows(recv_g, mat_g)

    def outer(i, carry):
        cols = pl.ds(pl.multiple_of(i * 384, 384), 384)
        tile = lax.dot_general(
            mat_g[:, cols], mat_h[...], (((0,), (0,)), ((), ())), preferred_element_type=F32
        )
        part[pl.ds(i * 2, 2)] = tile.reshape(2, 8, 3, 8, WIDE).astype(BF)
        return carry

    lax.fori_loop(0, 4, outer, 0)

    def e_copy(h):
        there = pl.ds(pl.multiple_of(h * 768 + (1 - c) * 384, 384), 384)
        return remote(
            part.at[:, :, :, :, there], sib.at[h], e_s.at[h], e_r.at[h], sibling
        )

    for h in range(2):
        e_copy(h).start()
    move_g.drain()

    def backward(j, carry):
        span = pl.ds(pl.multiple_of(j * 256, 256), 256)
        tile = jnp.dot(mat_g[...], mat_w[:, span], preferred_element_type=F32)
        send_g[:, :, :, :, span] = tile.reshape(4, 4, 5, 8, 256).astype(BF)
        return carry

    def local(h, b, n):
        here = pl.ds(pl.multiple_of(h * 768 + c * 384, 384), 384)
        return part[pl.ds(4 * n, 4), b, :, :, here].astype(F32) + sib[
            h, pl.ds(4 * n, 4), b
        ].astype(F32)

    def ring(h, s, n):
        some = pl.ds(4 * n, 4)
        if h == 0:
            return remote(
                ring_send.at[0, s, some], ring_recv.at[0, s, some],
                rp_s.at[n, s], rp_r.at[n, s], {"z": up},
            )
        return remote(
            ring_send.at[1, s, some], ring_recv.at[1, s, some],
            rm_s.at[n, s], rm_r.at[n, s], {"z": down},
        )

    def ring_step(s):
        for n in range(2):
            for h in range(2):
                some = pl.ds(4 * n, 4)
                b = lax.rem(z + 15 - s, 8) if h == 0 else lax.rem(z + 1 + s, 8)
                value = local(h, b, n)
                if s > 0:
                    ring(h, s - 1, n).wait_recv()
                    value = value + ring_recv[h, s - 1, some].astype(F32)
                ring_send[h, s, some] = value.astype(BF)
                ring(h, s, n).start()

    move_o.forward(1)
    lax.fori_loop(0, 3, backward, 0)
    move_o.forward(3)
    lax.fori_loop(3, 6, backward, 0)
    move_b.start()
    for h in range(2):
        e_copy(h).wait_recv()
    ring_step(0)
    move_o.forward(2)
    ring_step(1)
    ring_step(2)
    move_b.forward(1)
    ring_step(3)
    move_b.forward(3)
    ring_step(4)
    move_b.forward(2)

    move_o.arrive()

    def score_rows(i, carry):
        rows = pl.ds(pl.multiple_of(i * 80, 80), 80)
        value = home_out[i // 2, pl.ds(lax.rem(i, 2) * 2, 2)].astype(F32).reshape(80, WIDE)
        mat_h[rows, :] = value.astype(BF)
        score = jnp.sum(value * og_rows[rows, :].astype(F32), axis=1, keepdims=True)
        return carry + jnp.sum(
            jnp.where(sel[rows, :] > 0, score, 0.0), axis=0, keepdims=True
        )

    score_row = lax.fori_loop(0, 8, score_rows, jnp.zeros((1, SLOTS), F32))
    gate = gate_s[...]
    chosen_grad = gate * (score_row - group_sum(gate * score_row, lane))
    slot_table = jnp.where(pick_s[...] > 0, chosen_grad, 0.0)
    logit_grad = exact(slot_table, token_of, ((1,), (0,)))
    logit_half = logit_grad.astype(BF)
    bias_col = jnp.sum(logit_grad, axis=1, keepdims=True)
    table[:, pl.ds(2816, 256)] = jnp.zeros((EXPERTS, 256), F32)
    table[:, pl.ds(0, FEAT)] = lax.dot_general(
        logit_half, tokens[...], (((1,), (1,)), ((), ())), preferred_element_type=F32
    )

    def p_copy(k):
        px, py = offset(k, x, y)
        return remote(
            table.at[spot(px, py)], first.at[me], p_s.at[k], p_r.at[k], plane_id(px, py)
        )

    def q_copy(k):
        return remote(mine, second.at[zc], q_s.at[k], q_r.at[k], line(k))

    def t_copy(k):
        px, py = offset(k, x, y)
        return remote(
            done, total.at[spot(x, y)], t_s.at[k], t_r.at[k], plane_id(px, py)
        )

    each(lambda k: p_copy(k).start())
    first[me] = table[spot(x, y)]
    for s in range(5, 7):
        ring_step(s)
    load_b.wait()
    for n in range(2):
        for h in range(2):
            some = pl.ds(4 * n, 4)
            value = local(h, z, n)
            ring(h, 6, n).wait_recv()
            last[h, some] = (value + ring_recv[h, 6, some].astype(F32)).astype(BF)
    each(lambda k: l_copy(k).start())
    got[me] = last[yh, xy]

    each(lambda k: p_copy(k).wait_recv())
    mine[...] = jnp.sum(first[...], axis=0)
    each(lambda k: q_copy(k).start())
    second[zc] = mine[...]
    each(lambda k: l_copy(k).wait_recv())

    def coefficient(e, carry):
        prod = jnp.sum(got[map_s[e]].astype(F32) * src_b[e].astype(F32), axis=0)
        prods[e] = prod[:, :128] + prod[:, 128:256] + prod[:, 256:]
        return carry

    lax.fori_loop(0, EXPERTS, coefficient, 0)
    dots = jnp.sum(jnp.sum(prods[...], axis=1), axis=1, keepdims=True)
    at = iota((EXPERTS, 128), 1) == iota((EXPERTS, 128), 0)
    coef_row = jnp.sum(jnp.where(at, dots, 0.0), axis=0, keepdims=True)
    bias_row = jnp.sum(
        jnp.where(iota((EXPERTS, 128), 1) - 32 == iota((EXPERTS, 128), 0), bias_col, 0.0),
        axis=0, keepdims=True,
    )
    row_a[...] = jnp.broadcast_to(coef_row + bias_row, (8, 128))

    def u_copy(k):
        px, py = offset(k, x, y)
        return remote(row_a, row_b.at[me], u_s.at[k], u_r.at[k], plane_id(px, py))

    def v_copy(k):
        return remote(row_c, row_d.at[zc], v_s.at[k], v_r.at[k], line(k))

    each(lambda k: u_copy(k).start())
    row_b[me] = row_a[...]

    each(lambda k: q_copy(k).wait_recv())
    done[...] = jnp.sum(second[...], axis=0) * grad_scale
    each(lambda k: t_copy(k).start())
    total[spot(x, y)] = done[...]

    def expert(e, carry):
        expert_grad[e] = got[map_s[e]].astype(F32) * (coef_s[e] * grad_scale)
        return carry

    lax.fori_loop(0, EXPERTS, expert, 0)
    each(lambda k: u_copy(k).wait_recv())
    row_c[...] = jnp.sum(row_b[...], axis=0)
    each(lambda k: v_copy(k).start())
    row_d[zc] = row_c[...]
    token_grad[...] = lax.dot_general(
        router_t[...], logit_half, (((0,), (0,)), ((), ())), preferred_element_type=F32
    ).astype(BF)
    slot_token = iota((TOK, SLOTS), 1) // TOP == iota((TOK, SLOTS), 0)
    spread_gate = jnp.where(slot_token, gate, 0.0)
    high = spread_gate.astype(BF)
    low = (spread_gate - high.astype(F32)).astype(BF)

    def over_rows(v):
        return lax.dot_general(
            v, sel[...], (((1,), (1,)), ((), ())), preferred_element_type=F32
        ).astype(BF)

    mixed[...] = (
        jnp.dot(over_rows(high), mat_h[...], preferred_element_type=F32)
        + jnp.dot(over_rows(low), mat_h[...], preferred_element_type=F32)
    ).astype(BF)
    move_b.arrive()
    reshape_rows(home_back, mat_g)
    for j in range(6):
        span = pl.ds(j * 256, 256)
        tile = lax.dot_general(
            sel[...], mat_g[:, span], (((0,), (0,)), ((), ())), preferred_element_type=F32
        )
        hidden_grad[:, :, span] = tile.reshape(TOK, TOP, 256).astype(BF)
    each(lambda k: v_copy(k).wait_recv())
    small[...] = jnp.sum(row_d[...], axis=0) * grad_scale
    each(lambda k: t_copy(k).wait_recv())

    each(lambda k: a_copy(k).wait_send())
    for s in range(4):
        zp_copy(s).wait_send()
    for s in range(3):
        zm_copy(s).wait_send()
    for i in range(8):
        w_copy(i).wait_send()
    for h in range(2):
        e_copy(h).wait_send()
        for s in range(7):
            for n in range(2):
                ring(h, s, n).wait_send()
    move_o.drain()
    move_b.drain()
    each(lambda k: l_copy(k).wait_send())
    each(lambda k: p_copy(k).wait_send())
    each(lambda k: q_copy(k).wait_send())
    each(lambda k: t_copy(k).wait_send())
    each(lambda k: u_copy(k).wait_send())
    each(lambda k: v_copy(k).wait_send())


def finish_kernel(
    mixed, hidden_grad, token_grad, expert_grad, total, small,
    mixed_out, hidden_out, token_out, expert_out, router_out, bias_out, coef_out, sems,
):
    pairs = (
        (hidden_grad, hidden_out), (expert_grad, expert_out), (token_grad, token_out),
        (mixed, mixed_out),
    )
    copies = [pltpu.make_async_copy(a, b, sems.at[i]) for i, (a, b) in enumerate(pairs)]
    for copy in copies:
        copy.start()
    router_out[...] = total[:, pl.ds(0, FEAT)]
    row = small[pl.ds(0, 1), :]
    coef_out[...] = row[:, :EXPERTS]
    bias_out[...] = row[:, EXPERTS : 2 * EXPERTS]
    for copy in copies:
        copy.wait()


def finish(mixed, hidden_grad, token_grad, expert_grad, total, small):
    vmem = pl.BlockSpec(memory_space=pltpu.VMEM)
    hbm = pl.BlockSpec(memory_space=pl.ANY)
    like = lambda v: jax.ShapeDtypeStruct(v.shape, v.dtype)
    line = jax.ShapeDtypeStruct((1, EXPERTS), F32)
    return pl.pallas_call(
        finish_kernel,
        out_shape=(
            like(mixed), like(hidden_grad), like(token_grad), like(expert_grad),
            jax.ShapeDtypeStruct((EXPERTS, FEAT), F32), line, line,
        ),
        in_specs=[hbm] * 4 + [vmem] * 2,
        out_specs=(vmem,) * 7,
        scratch_shapes=[pltpu.SemaphoreType.DMA((4,))],
        name="finish",
    )(mixed, hidden_grad, token_grad, expert_grad, total, small)


def on_device(
    tokens, router_w, router_b, hidden, teacher_idx, merge_map, merge_coef, source_w, out_grad
):
    grad_scale = 1.0 / math.sqrt(TOK * 256)
    vmem = pl.BlockSpec(memory_space=pltpu.VMEM)
    smem = pl.BlockSpec(memory_space=pltpu.SMEM)
    dma = lambda n: pltpu.SemaphoreType.DMA((n,))
    rows = pltpu.VMEM((4, 4, 5, 8, WIDE), BF)
    relay = pltpu.VMEM((2, 3, 4, 5, 8, 768), BF)
    one = pltpu.SemaphoreType.DMA((2, 3))
    lap = pltpu.SemaphoreType.DMA((2, 7))
    two = pltpu.SemaphoreType.DMA((2, 4, 3))
    mat = pltpu.VMEM((ROWS, WIDE), BF)
    share = source_w.shape[1]

    def body(*refs):
        kernel(grad_scale, *refs)

    mixed, hidden_grad, token_grad, total, small, expert_grad = pl.pallas_call(
        body,
        out_shape=(
            jax.ShapeDtypeStruct((TOK, WIDE), BF),
            jax.ShapeDtypeStruct((TOK, TOP, WIDE), BF),
            jax.ShapeDtypeStruct((FEAT, TOK), BF),
            jax.ShapeDtypeStruct((EXPERTS, 3072), F32),
            jax.ShapeDtypeStruct((8, 128), F32),
            jax.ShapeDtypeStruct((EXPERTS, 3, 8, 384), F32),
        ),
        in_specs=[vmem] * 7 + [smem] * 2 + [pl.BlockSpec(memory_space=pl.ANY)],
        out_specs=(vmem,) * 6,
        scratch_shapes=[
            pltpu.VMEM((EXPERTS, 3, 8, 384), BF),
            pltpu.VMEM((EXPERTS, 3, 8, 384), BF),
            pltpu.VMEM((16, 3, 8, 384), BF),
            pltpu.VMEM((ROWS, SLOTS), BF),
            mat,
            pltpu.VMEM((1, SLOTS), F32),
            pltpu.VMEM((EXPERTS, SLOTS), F32),
            rows, rows,
            pltpu.VMEM((8, 8, 3, 8, WIDE), BF),
            rows, rows, mat, mat,
            pltpu.VMEM((WIDE, WIDE), BF),
            rows, rows,
            pltpu.VMEM((8, 8, 3, 8, WIDE), BF),
            pltpu.VMEM((2, 8, 8, 3, 8, 384), BF),
            pltpu.VMEM((2, 7, 8, 3, 8, 384), BF),
            pltpu.VMEM((2, 7, 8, 3, 8, 384), BF),
            pltpu.VMEM((2, 8, 3, 8, 384), BF),
            pltpu.VMEM((16, 3, 8, 384), BF),
            pltpu.VMEM((EXPERTS, 3072), F32),
            pltpu.VMEM((16, 8, 768), F32),
            pltpu.VMEM((8, 768), F32),
            pltpu.VMEM((16, 8, 768), F32),
            pltpu.VMEM((8, 768), F32),
            pltpu.VMEM((8, 128), F32),
            pltpu.VMEM((16, 8, 128), F32),
            pltpu.VMEM((8, 128), F32),
            pltpu.VMEM((16, 8, 128), F32),
            pltpu.VMEM((EXPERTS, 8, 128), F32),
            dma(2),
            dma(16), dma(16), dma(4), dma(4), dma(3), dma(3), dma(8), dma(8),
            dma(2), dma(2),
            lap, lap, lap, lap, dma(16), dma(16),
            dma(16), dma(16), dma(16), dma(16), dma(16), dma(16),
            dma(16), dma(16), dma(16), dma(16),
            relay, relay, relay, relay,
        ]
        + [one, one, two, two] * 4,
        compiler_params=pltpu.CompilerParams(
            collective_id=0, has_side_effects=True, vmem_limit_bytes=67043328
        ),
        name="whole",
    )(
        tokens[0].T,
        router_w.T,
        router_b.reshape(1, EXPERTS),
        hidden[0],
        teacher_idx[0].T,
        merge_map.reshape(1, EXPERTS),
        out_grad.reshape(TOK, WIDE),
        merge_map,
        merge_coef,
        source_w.reshape(EXPERTS, 3, 8, WIDE),
    )
    mixed, hidden_grad, token_grad, expert_grad, router, bias, coef = finish(
        mixed, hidden_grad, token_grad, expert_grad, total, small
    )
    return (
        mixed.reshape(1, TOK, WIDE),
        hidden_grad[None],
        token_grad.T[None],
        router.T,
        bias[0],
        coef[0],
        expert_grad.reshape(EXPERTS, share, 384),
    )


def solution(mesh):
    fine = jax.sharding.Mesh(mesh.devices.reshape(4, 2, 8, 2, 2), ("x", "yl", "z", "yh", "c"))
    ctx, rep = ("x", "yl", "z"), ("yh", "c")
    in_specs = (
        P(rep, ctx, None),
        P(),
        P(),
        P(rep, ctx, None, None),
        P(rep, ctx, None),
        P(),
        P(),
        P(None, ctx, None),
        P(rep, ctx, None),
    )
    out_specs = (
        P(rep, ctx, None),
        P(rep, ctx, None, None),
        P(rep, ctx, None),
        P(),
        P(),
        P(),
        P(None, ctx, rep),
    )
    return jax.shard_map(
        on_device, mesh=fine, in_specs=in_specs, out_specs=out_specs, check_vma=False
    )
```
